512 devices in a mesh: dom: 8 (over y_hi, core), slab: 64 (over y_lo, z, x).
Axes of the slice: x: 4, y: 8 (y_hi: 4, y_lo: 2; y = y_hi * 2 + y_lo), z: 8, core: 2. Of those that a mesh axis runs over, the one named last changes fastest.
Arguments:
- weights: bfloat16 [64, 256, 64, 128], P('slab', 'dom'), may hold values from 0 to 0.049804688
- moments: bfloat16 [64, 256, 10, 128], P('slab', 'dom'), may hold values from -6 to 6
- block_tile: int32 [64, 256], P('slab', 'dom'), may hold values from 0 to 255, as said below
- block_slab: int32 [64, 256], P('slab', 'dom'), may hold values from 0 to 63, as said below
- block_count: int32 [64, 8], P('slab', 'dom'), may hold values from 8 to 32, as said below
Outputs:
- filtered: float32 [10, 128, 64, 128], P(None, 'slab', 'dom')
The draws below stay inside these ranges and needn't reach their ends.
Inputs may be any that keep to these rules, and one draw needn't show every extreme that they name: Every device's used blocks are its first block_count slots; in every slab one device uses all 32 slots. `block_slab`: A block's target slab is its own slab or one of the two next to it on the periodic loop. `block_tile`: A block whose target is the next slab names a tile of that slab's first plane (tiles below 128); one whose target is the previous slab a tile of that slab's last plane (tiles from 128).
All inputs are finite; a program needn't handle non-finite values.
Results may differ from the reference program's by a relative error of at most 0.00035.
Values may be sent and summed in bfloat16 or wider, within the bound.
No kernel may reach another device: no remote copies, remote signals or barrier semaphores. Data moves between devices by JAX's collectives and lax.ppermute only.
A program may use at most 64 MiB of HBM per device.

```python
import jax
import jax.numpy as jnp
from jax import lax

MOM = 10
PB = 128
TC = 64
SX = 2
NZ = 128
BLK_DEV = 32
NY = 64
NX = 128
PT = 128
TILES = 256
BLOCKS = 256
N_DOM = 8
N_SLAB = 64


def routing_tables(key):
    base = jax.random.fold_in(key, 7)
    shape = (N_SLAB, N_DOM * BLK_DEV)
    kinds = jax.random.randint(jax.random.fold_in(base, 11), shape, 0, 4)
    column = jnp.arange(N_DOM * BLK_DEV, dtype=jnp.int32)[None, :]
    offset = jnp.where(kinds == 0, -1, jnp.where(kinds == 1, 1, 0))
    offset = jnp.where(column < 2, 0, offset)
    inner = jax.random.randint(jax.random.fold_in(base, 12), shape, 0, TILES)
    facing = jax.random.randint(jax.random.fold_in(base, 13), shape, 0, PT)
    tiles = jnp.where(offset == 0, inner, jnp.where(offset == 1, facing, (SX - 1) * PT + facing))
    tiles = jnp.where(column == 0, TILES - 1, jnp.where(column == 1, 0, tiles))
    slabs = jnp.mod(jnp.arange(N_SLAB, dtype=jnp.int32)[:, None] + offset, N_SLAB)
    return (tiles.astype(jnp.int32), slabs.astype(jnp.int32))


def draw_block_tile(key, part):
    return routing_tables(key)[0]


def draw_block_slab(key, part):
    return routing_tables(key)[1]


def draw_block_count(key, part):
    base = jax.random.fold_in(key, 29)
    counts = jax.random.randint(jax.random.fold_in(base, 1), (N_SLAB, N_DOM), max(1, BLK_DEV // 4), BLK_DEV // 2 + 1)
    fullest = jax.random.randint(jax.random.fold_in(base, 2), (N_SLAB, 1), 0, N_DOM)
    column = jnp.arange(N_DOM, dtype=jnp.int32)[None, :]
    return jnp.where(column == fullest, BLK_DEV, counts).astype(jnp.int32)


def level_of(own_key, shape, shards, low, top_value):
    def one(axis_at, blocks):
        heights = jax.random.uniform(jax.random.fold_in(jax.random.fold_in(own_key, 6), axis_at), (blocks,), jnp.float32, low / len(shards), top_value / len(shards))
        return jnp.repeat(jnp.exp(heights), shape[axis_at] // blocks).reshape((-1,) + (1,) * (len(shape) - axis_at - 1))

    gain = one(*shards[0])
    for cut in shards[1:]:
        gain = gain * one(*cut)
    return gain


def centred(own_key, dims, spread, limit, shards=(), held_as=jnp.bfloat16):
    array = spread * jax.random.normal(own_key, dims, jnp.float32)
    if shards:
        array = array * level_of(own_key, dims, shards, -0.22, 0.18)
    return jnp.clip(array, -limit, limit).astype(held_as)


def setup_inputs(seed: int = 0) -> dict:
    keys = jax.random.split(jax.random.key(seed), 6)
    return {
        "weights": jnp.clip(0.049804688 * jax.random.uniform(keys[0], (N_SLAB, BLOCKS, TC, PB), jnp.float32) ** level_of(keys[0], (N_SLAB, BLOCKS, TC, PB), ((0, 64), (1, 8)), -0.2, 0.2), 0.0, 0.049804688).astype(jnp.bfloat16),
        "moments": centred(keys[1], (N_SLAB, BLOCKS, MOM, PB), 1.0, 6.0, ((0, 64), (1, 8))),
        "block_tile": draw_block_tile(jax.random.fold_in(keys[5], 71), 0),
        "block_slab": draw_block_slab(jax.random.fold_in(keys[5], 71), 0),
        "block_count": draw_block_count(jax.random.fold_in(keys[5], 71), 0),
    }


def smooth_pass(field):
    adjacent_cell = jnp.roll(field, 1, axis=1) + jnp.roll(field, -1, axis=1)
    padded = jnp.pad(field, ((0, 0), (0, 0), (1, 1), (1, 1)))
    adjacent_cell = adjacent_cell + padded[:, :, 2:, 1:-1] + padded[:, :, :-2, 1:-1]
    adjacent_cell = adjacent_cell + padded[:, :, 1:-1, 2:] + padded[:, :, 1:-1, :-2]
    return field + 0.16 * (adjacent_cell - 6.0 * field)


def reference(weights, moments, block_tile, block_slab, block_count):
    slots = jnp.arange(BLOCKS, dtype=jnp.int32)
    slot_in_dev = slots % BLK_DEV
    device_of = slots // BLK_DEV

    def deposit_moments(grid, inputs):
        weight_blk, moment_blk, tile_blk, slab_blk, count_blk = inputs
        term_list = jnp.einsum("bmp,bcp->bmc", moment_blk.astype(jnp.float32), weight_blk.astype(jnp.float32))
        valid = (slot_in_dev < count_blk[device_of]).astype(jnp.float32)
        term_list = term_list * valid[:, None, None]
        target = (slab_blk * TILES + tile_blk).astype(jnp.int32)
        grid = grid.at[target].add(term_list.reshape(BLOCKS, MOM * TC))
        return grid, None

    start_grid = jnp.zeros((N_SLAB * TILES, MOM * TC), jnp.float32)
    grid, _ = lax.scan(deposit_moments, start_grid, (weights, moments, block_tile, block_slab, block_count))
    field = grid.reshape(NX, NY, NZ // TC, MOM, TC).transpose(3, 0, 1, 2, 4).reshape(MOM, NX, NY, NZ)
    field = smooth_pass(field)
    return smooth_pass(field)
```

```python
import jax
import jax.numpy as jnp
from jax import lax
from jax.experimental import pallas as pl
from jax.experimental.pallas import tpu as pltpu
from jax.sharding import PartitionSpec as P

MOM = 10
BLK = 32
TC = 64
NZ = 128
NY = 64
RY = 8
CHIP_ROWS = 2 * RY
HALO = 4
WIN = CHIP_ROWS + 2 * HALO
PLANES = 4
ROWS = 80
COLS = MOM * TC
diffusion = 0.16
keep_weight = 1.0 - 6.0 * diffusion


def iota(shape, dim):
    return lax.broadcasted_iota(jnp.int32, shape, dim)


def terms_kernel(place_ref, count_ref, tile_ref, slab_ref, weight_ref, moment_ref, out_ref, term_ref):
    my_slab, my_dom, n_slabs = place_ref[0], place_ref[1], place_ref[2]
    for b in range(BLK):
        w = weight_ref[b]
        both = jnp.concatenate([w, w], axis=0)
        term_ref[pl.ds(16 * b, MOM), :] = lax.dot_general(
            moment_ref[b], both, (((1,), (1,)), ((), ())), preferred_element_type=jnp.float32
        )
    low_half = iota((BLK, NZ), 1) < TC
    for j in range(MOM // 2):
        even = term_ref[pl.ds(2 * j, BLK, stride=16), :]
        odd = term_ref[pl.ds(2 * j + 1, BLK, stride=16), :]
        term = jnp.where(low_half, even, odd)
        high = term.astype(jnp.bfloat16)
        low = (term - high.astype(jnp.float32)).astype(jnp.bfloat16)
        out_ref[0:BLK, NZ * j : NZ * (j + 1)] = high
        out_ref[BLK : 2 * BLK, NZ * j : NZ * (j + 1)] = low
    tile, slab = tile_ref[...], slab_ref[...]
    step = slab - my_slab
    step = jnp.where(step == n_slabs - 1, -1, jnp.where(step == 1 - n_slabs, 1, step))
    plane = 1 + lax.shift_right_logical(tile, 7) + 2 * step
    row = lax.shift_right_logical(tile & 127, 1)
    used = iota((1, BLK), 1) < count_ref[0, 0]
    code = jnp.where(used, plane * NY + row + 1, 0).astype(jnp.float32).astype(jnp.bfloat16)
    half = (tile & 1).astype(jnp.float32).astype(jnp.bfloat16)
    slot = iota((BLK, COLS), 0)
    lane = iota((BLK, COLS), 1) - my_dom * ROWS
    spread = jnp.where((lane == slot) | (lane == slot + BLK), 1.0, 0.0).astype(jnp.bfloat16)
    code_row = jnp.dot(code, spread, preferred_element_type=jnp.float32)
    half_row = jnp.dot(half, spread, preferred_element_type=jnp.float32)
    sub = iota((ROWS - 2 * BLK, COLS), 0)
    codes = jnp.where(sub == 0, code_row, jnp.where(sub == 1, half_row, 0.0))
    out_ref[2 * BLK : ROWS, :] = codes.astype(jnp.bfloat16)


def field_kernel(place_ref, x_ref, first_ref, second_ref, own_ref, part_ref):
    my_slab, my_dom = place_ref[0], place_ref[1]
    core = lax.rem(my_dom, 2)
    top_row = (my_dom - core) * RY
    codes = x_ref[2 * BLK : ROWS, :].astype(jnp.float32)
    for k in range(1, 8):
        codes += x_ref[ROWS * k + 2 * BLK : ROWS * (k + 1), :].astype(jnp.float32)
    code = codes[0:1, :].astype(jnp.int32) - 1
    half = codes[1:2, :].astype(jnp.int32)
    plane = lax.shift_right_arithmetic(code, 6)
    rel = (code & (NY - 1)) - top_row
    valid = (code >= 0) & (rel >= -HALO) & (rel < CHIP_ROWS + HALO)
    spot = (half * PLANES + plane) * WIN + jnp.where(rel < 0, rel + WIN, rel)
    spot = jnp.where(valid, spot, -1)
    chosen = jnp.where(iota((2 * PLANES * WIN, COLS), 0) == spot, 1.0, 0.0).astype(jnp.bfloat16)
    cells = jnp.dot(chosen, x_ref[...], preferred_element_type=jnp.float32)

    lane = iota((WIN, NZ), 1)
    ring = iota((WIN, NZ), 0)
    at_row = top_row + jnp.where(ring < CHIP_ROWS + HALO, ring, ring - WIN)
    inside = (at_row >= 0) & (at_row < NY)

    def in_plane(f):
        z = jnp.where(lane == 0, 0.0, pltpu.roll(f, 1, 1)) + jnp.where(
            lane == NZ - 1, 0.0, pltpu.roll(f, NZ - 1, 1)
        )
        y = pltpu.roll(f, 1, 0) + pltpu.roll(f, WIN - 1, 0)
        return keep_weight * f + diffusion * (y + z)

    def filter_pass(planes):
        n = len(planes)
        out = []
        for i in range(-1, n + 1):
            value = in_plane(planes[i]) if 0 <= i < n else None
            for k in (i - 1, i + 1):
                if 0 <= k < n:
                    side = diffusion * planes[k]
                    value = side if value is None else value + side
            out.append(value)
        return out

    half_rows = PLANES * WIN
    for m in range(MOM):
        chunk = slice(NZ * (m // 2), NZ * (m // 2 + 1))
        planes = []
        for q in range(PLANES):
            lower = cells[WIN * q : WIN * (q + 1), chunk]
            upper = cells[half_rows + WIN * q : half_rows + WIN * (q + 1), chunk]
            if m % 2 == 0:
                upper = pltpu.roll(upper, TC, 1)
            else:
                lower = pltpu.roll(lower, TC, 1)
            planes.append(jnp.where(lane < TC, lower, upper))
        once = [jnp.where(inside, f, 0.0) for f in filter_pass(planes)]
        for i, f in enumerate(filter_pass(once)):
            part_ref[i, m, 0] = f[0:RY]
            part_ref[i, m, 1] = f[RY : 2 * RY]
    part_ref[8] = jnp.zeros((MOM, 2, RY, NZ), jnp.float32)

    for ref, odd_up in ((first_ref, 1), (second_ref, 0)):
        near_up = lax.rem(my_slab, 2) == odd_up
        far_up = lax.rem(lax.div(my_slab, 2), 2) == odd_up
        near = jnp.where(near_up, 5, 1)
        a = jnp.where(core == 1, near, jnp.where(far_up, 7, 8))
        b = jnp.where(core == 1, near + 1, jnp.where(far_up, 8, 0))
        for p, i in ((0, a), (1, b)):
            for h in range(2):
                ref[h, :, p] = part_ref[i, :, h]
    for p in range(2):
        own_ref[:, p] = part_ref[3 + p, :, core]


def swap_pairs(n_slabs, n_doms, odd_up):
    pairs = []
    for s in range(n_slabs):
        for d in range(n_doms):
            if d % 2 == 1:
                t = s + 1 if s % 2 == odd_up else s - 1
            else:
                t = s + 2 if (s // 2) % 2 == odd_up else s - 2
            pairs.append((d * n_slabs + s, d * n_slabs + t % n_slabs))
    return pairs


def local(weights, moments, block_tile, block_slab, block_count):
    n_slabs = lax.axis_size("slab")
    n_doms = lax.axis_size("dom")
    my_dom = lax.axis_index("dom")
    place = jnp.stack([lax.axis_index("slab"), my_dom, jnp.int32(n_slabs)]).astype(jnp.int32)
    smem = pl.BlockSpec(memory_space=pltpu.SMEM)
    vmem = pl.BlockSpec(memory_space=pltpu.VMEM)
    x = pl.pallas_call(
        terms_kernel,
        out_shape=jax.ShapeDtypeStruct((ROWS, COLS), jnp.bfloat16),
        in_specs=[smem, smem, vmem, vmem, vmem, vmem],
        out_specs=vmem,
        scratch_shapes=[pltpu.VMEM((16 * BLK, NZ), jnp.float32)],
        name="terms",
    )(place, block_count, block_tile, block_slab, weights[0], moments[0])
    gathered = lax.all_gather(x, "dom", tiled=True)
    message = jax.ShapeDtypeStruct((2, MOM, 2, RY, NZ), jnp.float32)
    first, second, own = pl.pallas_call(
        field_kernel,
        out_shape=(message, message, jax.ShapeDtypeStruct((MOM, 2, RY, NZ), jnp.float32)),
        in_specs=[smem, vmem],
        out_specs=(vmem, vmem, vmem),
        scratch_shapes=[pltpu.VMEM((9, MOM, 2, RY, NZ), jnp.float32)],
        name="field",
    )(place, gathered)
    first = lax.ppermute(first, ("dom", "slab"), swap_pairs(n_slabs, n_doms, 1))
    second = lax.ppermute(second, ("dom", "slab"), swap_pairs(n_slabs, n_doms, 0))
    arrived = first + second
    core = lax.rem(my_dom, 2)
    mine = lax.dynamic_index_in_dim(arrived, core, 0, keepdims=False) + own
    other = lax.dynamic_index_in_dim(arrived, 1 - core, 0, keepdims=False)
    other = lax.ppermute(other, "dom", [(i, i ^ 1) for i in range(n_doms)])
    return mine + other


def solution(mesh):
    return jax.shard_map(
        local,
        mesh=mesh,
        in_specs=(
            P("slab", "dom", None, None),
            P("slab", "dom", None, None),
            P("slab", "dom"),
            P("slab", "dom"),
            P("slab", "dom"),
        ),
        out_specs=P(None, "slab", "dom", None),
        check_vma=False,
    )
```

```python
import jax
import jax.numpy as jnp
from jax import lax
from jax.experimental import pallas as pl
from jax.experimental.pallas import tpu as pltpu
from jax.sharding import PartitionSpec as P

MOM = 10
BLK = 32
TC = 64
NZ = 128
NY = 64
RY = 8
CHIP_ROWS = 2 * RY
HALO = 4
WIN = CHIP_ROWS + 2 * HALO
PLANES = 4
ROWS = 80
COLS = MOM * TC
CHUNKS = 4
diffusion = 0.16
keep_weight = 1.0 - 6.0 * diffusion


def iota(shape, dim):
    return lax.broadcasted_iota(jnp.int32, shape, dim)


def terms_kernel(count_ref, tile_ref, slab_ref, weight_hbm, moment_ref, out_ref, weight_ref, term_ref, mom_ref, sems):
    my_slab, my_dom, n_slabs = lax.axis_index("slab"), lax.axis_index("dom"), lax.axis_size("slab")
    size = BLK // CHUNKS
    copies = []
    for c in range(CHUNKS):
        part = pl.ds(c * size, size)
        copies.append(pltpu.make_async_copy(weight_hbm.at[part], weight_ref.at[part], sems.at[c]))
        copies[c].start()
    for m in range(MOM):
        mom_ref[BLK * m : BLK * (m + 1), :] = moment_ref[m].astype(jnp.float32)
    tile, slab = tile_ref[...], slab_ref[...]
    step = slab - my_slab
    step = jnp.where(step == n_slabs - 1, -1, jnp.where(step == 1 - n_slabs, 1, step))
    plane = 1 + lax.shift_right_logical(tile, 7) + 2 * step
    row = lax.shift_right_logical(tile & 127, 1)
    used = iota((1, BLK), 1) < count_ref[0, 0]
    code = jnp.where(used, plane * NY + row + 1, 0).astype(jnp.float32)
    half = (tile & 1).astype(jnp.float32)
    both = jnp.where(iota((8, BLK), 0) == 0, code, half).astype(jnp.bfloat16)
    slot = iota((BLK, COLS), 0)
    lane = iota((BLK, COLS), 1) - my_dom * ROWS
    spread = jnp.where((lane == slot) | (lane == slot + BLK), 1.0, 0.0).astype(jnp.bfloat16)
    codes = jnp.dot(both, spread, preferred_element_type=jnp.float32).astype(jnp.bfloat16)
    out_ref[2 * BLK : ROWS, :] = jnp.concatenate([codes, codes], axis=0)
    for b in range(BLK):
        if b % size == 0:
            copies[b // size].wait()
        w = weight_ref[b]
        pair = jnp.concatenate([w, w], axis=0)
        mom = mom_ref[pl.ds(b, MOM, stride=BLK), :].astype(jnp.bfloat16)
        term_ref[pl.ds(16 * b, MOM), :] = lax.dot_general(
            mom, pair, (((1,), (1,)), ((), ())), preferred_element_type=jnp.float32
        )
    low_half = iota((BLK, NZ), 1) < TC
    for j in range(MOM // 2):
        even = term_ref[pl.ds(2 * j, BLK, stride=16), :]
        odd = term_ref[pl.ds(2 * j + 1, BLK, stride=16), :]
        term = jnp.where(low_half, even, odd)
        high = term.astype(jnp.bfloat16)
        low = (term - high.astype(jnp.float32)).astype(jnp.bfloat16)
        out_ref[0:BLK, NZ * j : NZ * (j + 1)] = high
        out_ref[BLK : 2 * BLK, NZ * j : NZ * (j + 1)] = low


def deposit(x_ref, top_row):
    codes = x_ref[2 * BLK : ROWS, :].astype(jnp.float32)
    for k in range(1, 8):
        codes += x_ref[ROWS * k + 2 * BLK : ROWS * (k + 1), :].astype(jnp.float32)
    code = codes[0:1, :].astype(jnp.int32) - 1
    half = codes[1:2, :].astype(jnp.int32)
    plane = lax.shift_right_arithmetic(code, 6)
    rel = (code & (NY - 1)) - top_row
    valid = (code >= 0) & (rel >= -HALO) & (rel < CHIP_ROWS + HALO)
    spot = (half * PLANES + plane) * WIN + jnp.where(rel < 0, rel + WIN, rel)
    spot = jnp.where(valid, spot, -1)
    chosen = jnp.where(iota((2 * PLANES * WIN, COLS), 0) == spot, 1.0, 0.0).astype(jnp.bfloat16)
    return jnp.dot(chosen, x_ref[...], preferred_element_type=jnp.float32)


class Stencil:
    def __init__(self, top_row):
        self.lane = iota((WIN, NZ), 1)
        ring = iota((WIN, NZ), 0)
        at_row = top_row + jnp.where(ring < CHIP_ROWS + HALO, ring, ring - WIN)
        self.inside = (at_row >= 0) & (at_row < NY)

    def planes(self, cells, m):
        chunk = slice(NZ * (m // 2), NZ * (m // 2 + 1))
        out = []
        for q in range(PLANES):
            lower = cells[WIN * q : WIN * (q + 1), chunk]
            upper = cells[WIN * (PLANES + q) : WIN * (PLANES + q + 1), chunk]
            if m % 2 == 0:
                upper = pltpu.roll(upper, TC, 1)
            else:
                lower = pltpu.roll(lower, TC, 1)
            out.append(jnp.where(self.lane < TC, lower, upper))
        return out

    def flat(self, f):
        z = jnp.where(self.lane == 0, 0.0, pltpu.roll(f, 1, 1)) + jnp.where(
            self.lane == NZ - 1, 0.0, pltpu.roll(f, NZ - 1, 1)
        )
        y = pltpu.roll(f, 1, 0) + pltpu.roll(f, WIN - 1, 0)
        return keep_weight * f + diffusion * (y + z)

    def kept(self, f):
        return jnp.where(self.inside, f, 0.0)


def send_kernel(x_ref, first_ref, second_ref, part_ref):
    my_slab, my_dom = lax.axis_index("slab"), lax.axis_index("dom")
    core = lax.rem(my_dom, 2)
    top_row = (my_dom - core) * RY
    cells = deposit(x_ref, top_row)
    st = Stencil(top_row)

    def put(i, m, f):
        part_ref[i, m, 0] = f[0:RY]
        part_ref[i, m, 1] = f[RY : 2 * RY]

    for m in range(MOM):
        g = st.planes(cells, m)
        put(0, m, diffusion * diffusion * g[0])
        put(5, m, diffusion * diffusion * g[3])

        def near(g0, g1, g2, i_far, i_near):
            l0 = st.flat(g0)
            once0 = st.kept(l0 + diffusion * g1)
            once1 = st.kept(st.flat(g1) + diffusion * (g0 + g2))
            put(i_far, m, diffusion * (l0 + once0))
            put(i_near, m, st.flat(once0) + diffusion * (diffusion * g0 + once1))

        near(g[0], g[1], g[2], 1, 2)
        near(g[3], g[2], g[1], 4, 3)
    part_ref[6] = jnp.zeros((MOM, 2, RY, NZ), jnp.float32)

    for ref, odd_up in ((first_ref, 1), (second_ref, 0)):
        near_up = lax.rem(my_slab, 2) == odd_up
        far_up = lax.rem(lax.div(my_slab, 2), 2) == odd_up
        at = jnp.where(near_up, 3, 1)
        a = jnp.where(core == 1, at, jnp.where(far_up, 5, 6))
        b = jnp.where(core == 1, at + 1, jnp.where(far_up, 6, 0))
        for p, i in ((0, a), (1, b)):
            for h in range(2):
                ref[h, :, p] = part_ref[i, :, h]


def own_kernel(x_ref, own_ref, part_ref):
    my_dom = lax.axis_index("dom")
    core = lax.rem(my_dom, 2)
    top_row = (my_dom - core) * RY
    cells = deposit(x_ref, top_row)
    st = Stencil(top_row)
    for m in range(MOM):
        g = st.planes(cells, m)
        flats = [st.flat(f) for f in g]
        once = [st.kept(flats[0] + diffusion * g[1])]
        once.append(st.kept(flats[1] + diffusion * (g[0] + g[2])))
        once.append(st.kept(flats[2] + diffusion * (g[1] + g[3])))
        once.append(st.kept(flats[3] + diffusion * g[2]))
        for p in range(2):
            f = st.flat(once[1 + p]) + diffusion * (once[p] + once[2 + p])
            part_ref[m, p, 0] = f[0:RY]
            part_ref[m, p, 1] = f[RY : 2 * RY]
    own_ref[...] = part_ref[:, :, core]


def swap_pairs(n_slabs, n_doms, odd_up):
    pairs = []
    for s in range(n_slabs):
        for d in range(n_doms):
            if d % 2 == 1:
                t = s + 1 if s % 2 == odd_up else s - 1
            else:
                t = s + 2 if (s // 2) % 2 == odd_up else s - 2
            pairs.append((d * n_slabs + s, d * n_slabs + t % n_slabs))
    return pairs


smem = pl.BlockSpec(memory_space=pltpu.SMEM)
vmem = pl.BlockSpec(memory_space=pltpu.VMEM)
anywhere = pl.BlockSpec(memory_space=pl.ANY)


def make_terms(weights, moments, block_tile, block_slab, block_count):
    return pl.pallas_call(
        terms_kernel,
        out_shape=jax.ShapeDtypeStruct((ROWS, COLS), jnp.bfloat16),
        in_specs=[smem, vmem, vmem, anywhere, vmem],
        out_specs=vmem,
        scratch_shapes=[
            pltpu.VMEM((BLK, TC, NZ), jnp.bfloat16),
            pltpu.VMEM((16 * BLK, NZ), jnp.float32),
            pltpu.VMEM((MOM * BLK, NZ), jnp.float32),
            pltpu.SemaphoreType.DMA((CHUNKS,)),
        ],
        name="terms",
    )(block_count, block_tile, block_slab, weights[0], moments[0].transpose(1, 0, 2))


def make_send(gathered):
    message = jax.ShapeDtypeStruct((2, MOM, 2, RY, NZ), jnp.float32)
    return pl.pallas_call(
        send_kernel,
        out_shape=(message, message),
        in_specs=[vmem],
        out_specs=(vmem, vmem),
        scratch_shapes=[pltpu.VMEM((7, MOM, 2, RY, NZ), jnp.float32)],
        name="send",
    )(gathered)


def make_own(gathered):
    return pl.pallas_call(
        own_kernel,
        out_shape=jax.ShapeDtypeStruct((MOM, 2, RY, NZ), jnp.float32),
        in_specs=[vmem],
        out_specs=vmem,
        scratch_shapes=[pltpu.VMEM((MOM, 2, 2, RY, NZ), jnp.float32)],
        cost_estimate=pl.CostEstimate(flops=400_000_000, bytes_accessed=8_000_000, transcendentals=0),
        name="own",
    )(gathered)


def local(weights, moments, block_tile, block_slab, block_count):
    n_slabs = lax.axis_size("slab")
    n_doms = lax.axis_size("dom")
    core = lax.rem(lax.axis_index("dom"), 2)
    x = make_terms(weights, moments, block_tile, block_slab, block_count)
    gathered = lax.all_gather(x, "dom", tiled=True)
    first, second = make_send(gathered)
    first = lax.ppermute(first, ("dom", "slab"), swap_pairs(n_slabs, n_doms, 1))
    second = lax.ppermute(second, ("dom", "slab"), swap_pairs(n_slabs, n_doms, 0))
    own = make_own(gathered)
    first, second, own = lax.optimization_barrier((first, second, own))
    arrived = first + second
    mine = lax.dynamic_index_in_dim(arrived, core, 0, keepdims=False) + own
    other = lax.dynamic_index_in_dim(arrived, 1 - core, 0, keepdims=False)
    other = lax.ppermute(other, "dom", [(i, i ^ 1) for i in range(n_doms)])
    return mine + other


def solution(mesh):
    return jax.shard_map(
        local,
        mesh=mesh,
        in_specs=(
            P("slab", "dom", None, None),
            P("slab", "dom", None, None),
            P("slab", "dom"),
            P("slab", "dom"),
            P("slab", "dom"),
        ),
        out_specs=P(None, "slab", "dom", None),
        check_vma=False,
    )
```

```python
import jax
import jax.numpy as jnp
from jax import lax
from jax.experimental import pallas as pl
from jax.experimental.pallas import tpu as pltpu
from jax.sharding import PartitionSpec as P

MOM = 10
BLK = 32
TC = 64
NZ = 128
NY = 64
RY = 8
CHIP_ROWS = 2 * RY
HALO = 4
WIN = CHIP_ROWS + 2 * HALO
PLANES = 4
ROWS = 80
COLS = MOM * TC
CHUNKS = 4
diffusion = 0.16
keep_weight = 1.0 - 6.0 * diffusion


def iota(shape, dim):
    return lax.broadcasted_iota(jnp.int32, shape, dim)


def terms_kernel(
    count_hbm, tile_hbm, slab_hbm, weight_hbm, moment_hbm, out_ref,
    count_ref, tile_ref, slab_ref, weight_ref, moment_ref, term_ref, mom_ref, sems,
):
    my_slab, my_dom, n_slabs = lax.axis_index("slab"), lax.axis_index("dom"), lax.axis_size("slab")
    size = BLK // CHUNKS
    small = [
        pltpu.make_async_copy(moment_hbm, moment_ref, sems.at[CHUNKS]),
        pltpu.make_async_copy(tile_hbm, tile_ref, sems.at[CHUNKS + 1]),
        pltpu.make_async_copy(slab_hbm, slab_ref, sems.at[CHUNKS + 2]),
        pltpu.make_async_copy(count_hbm, count_ref, sems.at[CHUNKS + 3]),
    ]
    copies = []
    for c in range(CHUNKS):
        part = pl.ds(c * size, size)
        copies.append(pltpu.make_async_copy(weight_hbm.at[part], weight_ref.at[part], sems.at[c]))
    for copy in small + copies:
        copy.start()
    for copy in small:
        copy.wait()
    for m in range(MOM):
        mom_ref[BLK * m : BLK * (m + 1), :] = moment_ref[m].astype(jnp.float32)
    tile, slab = tile_ref[...], slab_ref[...]
    step = slab - my_slab
    step = jnp.where(step == n_slabs - 1, -1, jnp.where(step == 1 - n_slabs, 1, step))
    plane = 1 + lax.shift_right_logical(tile, 7) + 2 * step
    row = lax.shift_right_logical(tile & 127, 1)
    used = iota((1, BLK), 1) < count_ref[...]
    code = jnp.where(used, plane * NY + row + 1, 0).astype(jnp.float32)
    half = (tile & 1).astype(jnp.float32)
    both = jnp.where(iota((8, BLK), 0) == 0, code, half).astype(jnp.bfloat16)
    slot = iota((BLK, COLS), 0)
    lane = iota((BLK, COLS), 1) - my_dom * ROWS
    spread = jnp.where((lane == slot) | (lane == slot + BLK), 1.0, 0.0).astype(jnp.bfloat16)
    codes = jnp.dot(both, spread, preferred_element_type=jnp.float32).astype(jnp.bfloat16)
    out_ref[2 * BLK : ROWS, :] = jnp.concatenate([codes, codes], axis=0)
    for b in range(BLK):
        if b % size == 0:
            copies[b // size].wait()
        w = weight_ref[b]
        pair = jnp.concatenate([w, w], axis=0)
        mom = mom_ref[pl.ds(b, MOM, stride=BLK), :].astype(jnp.bfloat16)
        term_ref[pl.ds(16 * b, MOM), :] = lax.dot_general(
            mom, pair, (((1,), (1,)), ((), ())), preferred_element_type=jnp.float32
        )
    low_half = iota((BLK, NZ), 1) < TC
    for j in range(MOM // 2):
        even = term_ref[pl.ds(2 * j, BLK, stride=16), :]
        odd = term_ref[pl.ds(2 * j + 1, BLK, stride=16), :]
        term = jnp.where(low_half, even, odd)
        high = term.astype(jnp.bfloat16)
        low = (term - high.astype(jnp.float32)).astype(jnp.bfloat16)
        out_ref[0:BLK, NZ * j : NZ * (j + 1)] = high
        out_ref[BLK : 2 * BLK, NZ * j : NZ * (j + 1)] = low


def deposit(x_ref, top_row):
    codes = x_ref[2 * BLK : ROWS, :].astype(jnp.float32)
    for k in range(1, 8):
        codes += x_ref[ROWS * k + 2 * BLK : ROWS * (k + 1), :].astype(jnp.float32)
    code = codes[0:1, :].astype(jnp.int32) - 1
    half = codes[1:2, :].astype(jnp.int32)
    plane = lax.shift_right_arithmetic(code, 6)
    rel = (code & (NY - 1)) - top_row
    valid = (code >= 0) & (rel >= -HALO) & (rel < CHIP_ROWS + HALO)
    spot = (half * PLANES + plane) * WIN + jnp.where(rel < 0, rel + WIN, rel)
    spot = jnp.where(valid, spot, -1)
    chosen = jnp.where(iota((2 * PLANES * WIN, COLS), 0) == spot, 1.0, 0.0).astype(jnp.bfloat16)
    return jnp.dot(chosen, x_ref[...], preferred_element_type=jnp.float32)


class Stencil:
    def __init__(self, top_row):
        self.lane = iota((WIN, NZ), 1)
        ring = iota((WIN, NZ), 0)
        at_row = top_row + jnp.where(ring < CHIP_ROWS + HALO, ring, ring - WIN)
        self.inside = (at_row >= 0) & (at_row < NY)

    def planes(self, cells, m):
        chunk = slice(NZ * (m // 2), NZ * (m // 2 + 1))
        out = []
        for q in range(PLANES):
            lower = cells[WIN * q : WIN * (q + 1), chunk]
            upper = cells[WIN * (PLANES + q) : WIN * (PLANES + q + 1), chunk]
            if m % 2 == 0:
                upper = pltpu.roll(upper, TC, 1)
            else:
                lower = pltpu.roll(lower, TC, 1)
            out.append(jnp.where(self.lane < TC, lower, upper))
        return out

    def flat(self, f):
        z = jnp.where(self.lane == 0, 0.0, pltpu.roll(f, 1, 1)) + jnp.where(
            self.lane == NZ - 1, 0.0, pltpu.roll(f, NZ - 1, 1)
        )
        y = pltpu.roll(f, 1, 0) + pltpu.roll(f, WIN - 1, 0)
        return keep_weight * f + diffusion * (y + z)

    def kept(self, f):
        return jnp.where(self.inside, f, 0.0)


def send_kernel(x_ref, early_ref, outer_ref, late_ref, part_ref):
    my_slab, my_dom = lax.axis_index("slab"), lax.axis_index("dom")
    core = lax.rem(my_dom, 2)
    top_row = (my_dom - core) * RY
    cells = deposit(x_ref, top_row)
    st = Stencil(top_row)

    def put(i, m, f):
        part_ref[i, m, 0] = f[0:RY]
        part_ref[i, m, 1] = f[RY : 2 * RY]

    for m in range(MOM):
        g = st.planes(cells, m)
        put(0, m, diffusion * diffusion * g[0])
        put(5, m, diffusion * diffusion * g[3])

        def near(g0, g1, g2, i_far, i_near):
            l0 = st.flat(g0)
            once0 = st.kept(l0 + diffusion * g1)
            once1 = st.kept(st.flat(g1) + diffusion * (g0 + g2))
            put(i_far, m, diffusion * (l0 + once0))
            put(i_near, m, st.flat(once0) + diffusion * (diffusion * g0 + once1))

        near(g[0], g[1], g[2], 1, 2)
        near(g[3], g[2], g[1], 4, 3)
    part_ref[6] = jnp.zeros((MOM, 2, RY, NZ), jnp.float32)

    for refs, odd_up in (((outer_ref,), 1), ((early_ref, late_ref), 0)):
        near_up = lax.rem(my_slab, 2) == odd_up
        far_up = lax.rem(lax.div(my_slab, 2), 2) == odd_up
        at = jnp.where(near_up, 3, 1)
        a = jnp.where(core == 1, at, jnp.where(far_up, 5, 6))
        b = jnp.where(core == 1, at + 1, jnp.where(far_up, 6, 0))
        for p, i in ((0, a), (1, b)):
            for h in range(2):
                for ref in refs:
                    ref[h, :, p] = part_ref[i, :, h]


def own_kernel(x_ref, own_ref, part_ref):
    my_dom = lax.axis_index("dom")
    core = lax.rem(my_dom, 2)
    top_row = (my_dom - core) * RY
    cells = deposit(x_ref, top_row)
    st = Stencil(top_row)
    for m in range(MOM):
        g = st.planes(cells, m)
        flats = [st.flat(f) for f in g]
        once = [st.kept(flats[0] + diffusion * g[1])]
        once.append(st.kept(flats[1] + diffusion * (g[0] + g[2])))
        once.append(st.kept(flats[2] + diffusion * (g[1] + g[3])))
        once.append(st.kept(flats[3] + diffusion * g[2]))
        for p in range(2):
            f = st.flat(once[1 + p]) + diffusion * (once[p] + once[2 + p])
            part_ref[m, p, 0] = f[0:RY]
            part_ref[m, p, 1] = f[RY : 2 * RY]
    own_ref[...] = part_ref[:, :, core]


def swap_pairs(n_slabs, n_doms, odd_up, chosen):
    pairs = []
    for s in range(n_slabs):
        for d in range(n_doms):
            if not chosen(s):
                continue
            if d % 2 == 1:
                t = s + 1 if s % 2 == odd_up else s - 1
            else:
                t = s + 2 if (s // 2) % 2 == odd_up else s - 2
            pairs.append((d * n_slabs + s, d * n_slabs + t % n_slabs))
    return pairs


limited = pltpu.CompilerParams(vmem_limit_bytes=16 * 1024 * 1024)
alone = pltpu.CompilerParams(vmem_limit_bytes=60 * 1024 * 1024)
hbm = pl.BlockSpec(memory_space=pltpu.HBM)
vmem = pl.BlockSpec(memory_space=pltpu.VMEM)


def make_terms(weights, moments, block_tile, block_slab, block_count):
    return pl.pallas_call(
        terms_kernel,
        out_shape=jax.ShapeDtypeStruct((ROWS, COLS), jnp.bfloat16),
        in_specs=[hbm] * 5,
        out_specs=vmem,
        scratch_shapes=[
            pltpu.VMEM((1, 1), jnp.int32),
            pltpu.VMEM((1, BLK), jnp.int32),
            pltpu.VMEM((1, BLK), jnp.int32),
            pltpu.VMEM((BLK, TC, NZ), jnp.bfloat16),
            pltpu.VMEM((MOM, BLK, NZ), jnp.bfloat16),
            pltpu.VMEM((16 * BLK, NZ), jnp.float32),
            pltpu.VMEM((MOM * BLK, NZ), jnp.float32),
            pltpu.SemaphoreType.DMA((CHUNKS + 4,)),
        ],
        compiler_params=alone,
        name="terms",
    )(block_count, block_tile, block_slab, weights[0], moments[0].transpose(1, 0, 2))


def make_send(gathered):
    message = jax.ShapeDtypeStruct((2, MOM, 2, RY, NZ), jnp.float32)
    return pl.pallas_call(
        send_kernel,
        out_shape=(message,) * 3,
        in_specs=[vmem],
        out_specs=(vmem,) * 3,
        scratch_shapes=[pltpu.VMEM((7, MOM, 2, RY, NZ), jnp.float32)],
        compiler_params=limited,
        name="send",
    )(gathered)


def make_own(gathered):
    return pl.pallas_call(
        own_kernel,
        out_shape=jax.ShapeDtypeStruct((MOM, 2, RY, NZ), jnp.float32),
        in_specs=[vmem],
        out_specs=vmem,
        scratch_shapes=[pltpu.VMEM((MOM, 2, 2, RY, NZ), jnp.float32)],
        cost_estimate=pl.CostEstimate(flops=400_000_000, bytes_accessed=8_000_000, transcendentals=0),
        compiler_params=limited,
        name="own",
    )(gathered)


def local(weights, moments, block_tile, block_slab, block_count):
    n_slabs = lax.axis_size("slab")
    n_doms = lax.axis_size("dom")
    core = lax.rem(lax.axis_index("dom"), 2)
    x = make_terms(weights, moments, block_tile, block_slab, block_count)
    gathered = lax.all_gather(x, "dom", tiled=True)
    early, outer, late = make_send(gathered)
    both = ("dom", "slab")
    half = lambda low: lambda s: ((s // 4) % 8 < 4) == low
    early = lax.ppermute(early, both, swap_pairs(n_slabs, n_doms, 0, half(True)))
    outer = lax.ppermute(outer, both, swap_pairs(n_slabs, n_doms, 1, lambda s: True))
    late = lax.ppermute(late, both, swap_pairs(n_slabs, n_doms, 0, half(False)))
    own = make_own(gathered)
    early, outer, late, own = lax.optimization_barrier((early, outer, late, own))
    arrived = outer + (early + late)
    mine = lax.dynamic_index_in_dim(arrived, core, 0, keepdims=False) + own
    other = lax.dynamic_index_in_dim(arrived, 1 - core, 0, keepdims=False)
    other = lax.ppermute(other, "dom", [(i, i ^ 1) for i in range(n_doms)])
    return mine + other


def solution(mesh):
    return jax.shard_map(
        local,
        mesh=mesh,
        in_specs=(
            P("slab", "dom", None, None),
            P("slab", "dom", None, None),
            P("slab", "dom"),
            P("slab", "dom"),
            P("slab", "dom"),
        ),
        out_specs=P(None, "slab", "dom", None),
        check_vma=False,
    )
```

```python
import functools

import jax
import jax.numpy as jnp
from jax import lax
from jax.experimental import pallas as pl
from jax.experimental.pallas import tpu as pltpu
from jax.sharding import PartitionSpec as P

MOM = 10
BLK = 32
TC = 64
NZ = 128
NY = 64
RY = 8
CHIP_ROWS = 2 * RY
HALO = 4
WIN = CHIP_ROWS + 2 * HALO
PLANES = 4
ROWS = 80
COLS = MOM * TC
CHUNKS = 4
diffusion = 0.16
keep_weight = 1.0 - 6.0 * diffusion


def iota(shape, dim):
    return lax.broadcasted_iota(jnp.int32, shape, dim)


def fixed_factor(top):
    return jnp.exp2(14.9 - top)


def terms_kernel(
    count_ref, tile_hbm, slab_hbm, weight_hbm, moment_hbm, out_ref,
    tile_ref, slab_ref, weight_ref, moment_ref, term_ref, mom_ref, sems,
):
    my_slab, my_dom, n_slabs = lax.axis_index("slab"), lax.axis_index("dom"), lax.axis_size("slab")
    size = BLK // CHUNKS
    small = [
        pltpu.make_async_copy(moment_hbm, moment_ref, sems.at[CHUNKS]),
        pltpu.make_async_copy(tile_hbm, tile_ref, sems.at[CHUNKS + 1]),
        pltpu.make_async_copy(slab_hbm, slab_ref, sems.at[CHUNKS + 2]),
    ]
    copies = []
    for c in range(CHUNKS):
        part = pl.ds(c * size, size)
        copies.append(pltpu.make_async_copy(weight_hbm.at[part], weight_ref.at[part], sems.at[c]))
    for copy in small + copies:
        copy.start()
    for copy in small:
        copy.wait()
    for m in range(MOM):
        mom_ref[BLK * m : BLK * (m + 1), :] = moment_ref[m].astype(jnp.float32)
    tile, slab = tile_ref[...], slab_ref[...]
    step = slab - my_slab
    step = jnp.where(step == n_slabs - 1, -1, jnp.where(step == 1 - n_slabs, 1, step))
    plane = 1 + lax.shift_right_logical(tile, 7) + 2 * step
    row = lax.shift_right_logical(tile & 127, 1)
    used = iota((1, BLK), 1) < count_ref[0, 0]
    code = jnp.where(used, plane * NY + row + 1, 0).astype(jnp.float32)
    half = (tile & 1).astype(jnp.float32)
    both = jnp.where(iota((8, BLK), 0) == 0, code, half).astype(jnp.bfloat16)
    slot = iota((BLK, COLS), 0)
    lane = iota((BLK, COLS), 1) - my_dom * ROWS
    spread = jnp.where((lane == slot) | (lane == slot + BLK), 1.0, 0.0).astype(jnp.bfloat16)
    codes = jnp.dot(both, spread, preferred_element_type=jnp.float32).astype(jnp.bfloat16)
    out_ref[2 * BLK : ROWS, :] = jnp.concatenate([codes, codes], axis=0)
    for b in range(BLK):
        if b % size == 0:
            copies[b // size].wait()
        w = weight_ref[b]
        pair = jnp.concatenate([w, w], axis=0)
        mom = mom_ref[pl.ds(b, MOM, stride=BLK), :].astype(jnp.bfloat16)
        term_ref[pl.ds(16 * b, MOM), :] = lax.dot_general(
            mom, pair, (((1,), (1,)), ((), ())), preferred_element_type=jnp.float32
        )
    low_half = iota((BLK, NZ), 1) < TC
    for j in range(MOM // 2):
        even = term_ref[pl.ds(2 * j, BLK, stride=16), :]
        odd = term_ref[pl.ds(2 * j + 1, BLK, stride=16), :]
        term = jnp.where(low_half, even, odd)
        high = term.astype(jnp.bfloat16)
        low = (term - high.astype(jnp.float32)).astype(jnp.bfloat16)
        out_ref[0:BLK, NZ * j : NZ * (j + 1)] = high
        out_ref[BLK : 2 * BLK, NZ * j : NZ * (j + 1)] = low


def deposit(x_ref, top_row):
    codes = x_ref[2 * BLK : ROWS, :].astype(jnp.float32)
    for k in range(1, 8):
        codes += x_ref[ROWS * k + 2 * BLK : ROWS * (k + 1), :].astype(jnp.float32)
    code = codes[0:1, :].astype(jnp.int32) - 1
    half = codes[1:2, :].astype(jnp.int32)
    plane = lax.shift_right_arithmetic(code, 6)
    rel = (code & (NY - 1)) - top_row
    valid = (code >= 0) & (rel >= -HALO) & (rel < CHIP_ROWS + HALO)
    spot = (half * PLANES + plane) * WIN + jnp.where(rel < 0, rel + WIN, rel)
    spot = jnp.where(valid, spot, -1)
    chosen = jnp.where(iota((2 * PLANES * WIN, COLS), 0) == spot, 1.0, 0.0).astype(jnp.bfloat16)
    return jnp.dot(chosen, x_ref[...], preferred_element_type=jnp.float32)


class Stencil:
    def __init__(self, top_row):
        self.lane = iota((WIN, NZ), 1)
        ring = iota((WIN, NZ), 0)
        at_row = top_row + jnp.where(ring < CHIP_ROWS + HALO, ring, ring - WIN)
        self.inside = (at_row >= 0) & (at_row < NY)

    def planes(self, cells, m):
        chunk = slice(NZ * (m // 2), NZ * (m // 2 + 1))
        out = []
        for q in range(PLANES):
            lower = cells[WIN * q : WIN * (q + 1), chunk]
            upper = cells[WIN * (PLANES + q) : WIN * (PLANES + q + 1), chunk]
            if m % 2 == 0:
                upper = pltpu.roll(upper, TC, 1)
            else:
                lower = pltpu.roll(lower, TC, 1)
            out.append(jnp.where(self.lane < TC, lower, upper))
        return out

    def flat(self, f):
        z = jnp.where(self.lane == 0, 0.0, pltpu.roll(f, 1, 1)) + jnp.where(
            self.lane == NZ - 1, 0.0, pltpu.roll(f, NZ - 1, 1)
        )
        y = pltpu.roll(f, 1, 0) + pltpu.roll(f, WIN - 1, 0)
        return keep_weight * f + diffusion * (y + z)

    def kept(self, f):
        return jnp.where(self.inside, f, 0.0)


def send_kernel(x_ref, early_ref, outer_ref, late_ref, part_ref):
    my_slab, my_dom = lax.axis_index("slab"), lax.axis_index("dom")
    core = lax.rem(my_dom, 2)
    top_row = (my_dom - core) * RY
    cells = deposit(x_ref, top_row)
    st = Stencil(top_row)

    def put(i, m, f):
        part_ref[i, m, 0] = f[0:RY]
        part_ref[i, m, 1] = f[RY : 2 * RY]

    for m in range(MOM):
        g = st.planes(cells, m)
        put(0, m, diffusion * diffusion * g[0])
        put(5, m, diffusion * diffusion * g[3])

        def near(g0, g1, g2, i_far, i_near):
            l0 = st.flat(g0)
            once0 = st.kept(l0 + diffusion * g1)
            once1 = st.kept(st.flat(g1) + diffusion * (g0 + g2))
            put(i_far, m, diffusion * (l0 + once0))
            put(i_near, m, st.flat(once0) + diffusion * (diffusion * g0 + once1))

        near(g[0], g[1], g[2], 1, 2)
        near(g[3], g[2], g[1], 4, 3)
    part_ref[6] = jnp.zeros((MOM, 2, RY, NZ), jnp.float32)

    sub = iota((RY, NZ), 0)
    for refs, odd_up in (((outer_ref,), 1), ((early_ref, late_ref), 0)):
        near_up = lax.rem(my_slab, 2) == odd_up
        far_up = lax.rem(lax.div(my_slab, 2), 2) == odd_up
        at = jnp.where(near_up, 3, 1)
        a = jnp.where(core == 1, at, jnp.where(far_up, 5, 6))
        b = jnp.where(core == 1, at + 1, jnp.where(far_up, 6, 0))
        tops = [jnp.zeros((RY, NZ), jnp.float32)] * 2
        for m in range(MOM):
            values = [part_ref[i, m, h] for h in range(2) for i in (a, b)]
            top = functools.reduce(jnp.maximum, [jnp.abs(v) for v in values])
            for k in (4, 2, 1):
                top = jnp.maximum(top, pltpu.roll(top, k, 0))
            top = jnp.floor(jnp.log2(jnp.maximum(top, 1e-30))) + 1.0
            factor = fixed_factor(top)
            tops[m // RY] = jnp.where(sub == m % RY, top, tops[m // RY])
            for k, v in enumerate(values):
                q = jnp.floor(v * factor + 0.5).astype(jnp.int32).astype(jnp.int16)
                for ref in refs:
                    ref[4 * m + k] = q
        for k in range(2):
            q = tops[k].astype(jnp.int32).astype(jnp.int16)
            for ref in refs:
                ref[4 * MOM + k] = q


def join_kernel(early_ref, outer_ref, late_ref, own_ref, mine_ref, other_ref):
    core = lax.rem(lax.axis_index("dom"), 2)
    refs = (early_ref, outer_ref, late_ref)
    tops = [[ref[4 * MOM + k].astype(jnp.float32) for k in range(2)] for ref in refs]
    for m in range(MOM):
        at = m % RY
        scales = [1.0 / fixed_factor(top[m // RY][at : at + 1]) for top in tops]
        for p in range(2):

            def arrived(h):
                parts = [ref[4 * m + 2 * h + p].astype(jnp.float32) * c for ref, c in zip(refs, scales)]
                return parts[0] + parts[1] + parts[2]

            other_ref[m, p] = arrived(1 - core)
            mine_ref[m, p] = own_ref[m, p] + arrived(core)


def own_kernel(x_ref, own_ref, part_ref):
    my_dom = lax.axis_index("dom")
    core = lax.rem(my_dom, 2)
    top_row = (my_dom - core) * RY
    cells = deposit(x_ref, top_row)
    st = Stencil(top_row)
    for m in range(MOM):
        g = st.planes(cells, m)
        flats = [st.flat(f) for f in g]
        once = [st.kept(flats[0] + diffusion * g[1])]
        once.append(st.kept(flats[1] + diffusion * (g[0] + g[2])))
        once.append(st.kept(flats[2] + diffusion * (g[1] + g[3])))
        once.append(st.kept(flats[3] + diffusion * g[2]))
        for p in range(2):
            f = st.flat(once[1 + p]) + diffusion * (once[p] + once[2 + p])
            part_ref[m, p, 0] = f[0:RY]
            part_ref[m, p, 1] = f[RY : 2 * RY]
    own_ref[...] = part_ref[:, :, core]


def swap_pairs(n_slabs, n_doms, odd_up, chosen):
    pairs = []
    for s in range(n_slabs):
        for d in range(n_doms):
            if not chosen(s):
                continue
            if d % 2 == 1:
                t = s + 1 if s % 2 == odd_up else s - 1
            else:
                t = s + 2 if (s // 2) % 2 == odd_up else s - 2
            pairs.append((d * n_slabs + s, d * n_slabs + t % n_slabs))
    return pairs


limited = pltpu.CompilerParams(vmem_limit_bytes=16 * 1024 * 1024)
alone = pltpu.CompilerParams(vmem_limit_bytes=60 * 1024 * 1024)
smem = pl.BlockSpec(memory_space=pltpu.SMEM)
hbm = pl.BlockSpec(memory_space=pltpu.HBM)
vmem = pl.BlockSpec(memory_space=pltpu.VMEM)


def make_terms(weights, moments, block_tile, block_slab, block_count):
    return pl.pallas_call(
        terms_kernel,
        out_shape=pltpu.VMEM((ROWS, COLS), jnp.bfloat16),
        in_specs=[smem] + [hbm] * 4,
        out_specs=vmem,
        scratch_shapes=[
            pltpu.VMEM((1, BLK), jnp.int32),
            pltpu.VMEM((1, BLK), jnp.int32),
            pltpu.VMEM((BLK, TC, NZ), jnp.bfloat16),
            pltpu.VMEM((MOM, BLK, NZ), jnp.bfloat16),
            pltpu.VMEM((16 * BLK, NZ), jnp.float32),
            pltpu.VMEM((MOM * BLK, NZ), jnp.float32),
            pltpu.SemaphoreType.DMA((CHUNKS + 3,)),
        ],
        compiler_params=alone,
        name="terms",
    )(block_count, block_tile, block_slab, weights[0], moments[0].transpose(1, 0, 2))


def make_send(gathered):
    message = jax.ShapeDtypeStruct((4 * MOM + 2, RY, NZ), jnp.int16)
    return pl.pallas_call(
        send_kernel,
        out_shape=(message,) * 3,
        in_specs=[vmem],
        out_specs=(vmem,) * 3,
        scratch_shapes=[pltpu.VMEM((7, MOM, 2, RY, NZ), jnp.float32)],
        compiler_params=limited,
        name="send",
    )(gathered)


def make_own(gathered):
    return pl.pallas_call(
        own_kernel,
        out_shape=jax.ShapeDtypeStruct((MOM, 2, RY, NZ), jnp.float32),
        in_specs=[vmem],
        out_specs=vmem,
        scratch_shapes=[pltpu.VMEM((MOM, 2, 2, RY, NZ), jnp.float32)],
        cost_estimate=pl.CostEstimate(flops=400_000_000, bytes_accessed=8_000_000, transcendentals=0),
        compiler_params=limited,
        name="own",
    )(gathered)


def local(weights, moments, block_tile, block_slab, block_count):
    n_slabs = lax.axis_size("slab")
    n_doms = lax.axis_size("dom")
    x = make_terms(weights, moments, block_tile, block_slab, block_count)
    gathered = lax.all_gather(x, "dom", tiled=True)
    early, outer, late = make_send(gathered)
    both = ("dom", "slab")
    half = lambda low: lambda s: ((s // 4) % 8 < 4) == low
    early = lax.ppermute(early, both, swap_pairs(n_slabs, n_doms, 0, half(True)))
    outer = lax.ppermute(outer, both, swap_pairs(n_slabs, n_doms, 1, lambda s: True))
    late = lax.ppermute(late, both, swap_pairs(n_slabs, n_doms, 0, half(False)))
    own = make_own(gathered)
    early, outer, late, own = lax.optimization_barrier((early, outer, late, own))
    part = jax.ShapeDtypeStruct((MOM, 2, RY, NZ), jnp.float32)
    mine, other = pl.pallas_call(
        join_kernel,
        out_shape=(part, part),
        in_specs=[vmem] * 4,
        out_specs=(vmem, vmem),
        compiler_params=limited,
        name="join",
    )(early, outer, late, own)
    other = lax.ppermute(other, "dom", [(i, i ^ 1) for i in range(n_doms)])
    return mine + other


def solution(mesh):
    return jax.shard_map(
        local,
        mesh=mesh,
        in_specs=(
            P("slab", "dom", None, None),
            P("slab", "dom", None, None),
            P("slab", "dom"),
            P("slab", "dom"),
            P("slab", "dom"),
        ),
        out_specs=P(None, "slab", "dom", None),
        check_vma=False,
    )
```

```python
import functools

import jax
import jax.numpy as jnp
from jax import lax
from jax.experimental import pallas as pl
from jax.experimental.pallas import tpu as pltpu
from jax.sharding import PartitionSpec as P

MOM = 10
BLK = 32
TC = 64
NZ = 128
NY = 64
RY = 8
CHIP_ROWS = 2 * RY
HALO = 4
WIN = CHIP_ROWS + 2 * HALO
PLANES = 4
ROWS = 80
COLS = MOM * TC
KEPT = 8 * 2 * BLK
CHUNKS = 2
GROUP = 4
diffusion = 0.16
keep_weight = 1.0 - 6.0 * diffusion


def iota(shape, dim):
    return lax.broadcasted_iota(jnp.int32, shape, dim)


def fixed_factor(top):
    return jnp.exp2(14.9 - top)


def terms_kernel(
    count_ref, tile_hbm, slab_hbm, weight_hbm, moment_hbm, out_ref,
    tile_ref, slab_ref, weight_ref, moment_ref, term_ref, mom_ref, sems,
):
    my_slab, my_dom, n_slabs = lax.axis_index("slab"), lax.axis_index("dom"), lax.axis_size("slab")
    size = BLK // CHUNKS
    small = [
        pltpu.make_async_copy(moment_hbm, moment_ref, sems.at[CHUNKS]),
        pltpu.make_async_copy(tile_hbm, tile_ref, sems.at[CHUNKS + 1]),
        pltpu.make_async_copy(slab_hbm, slab_ref, sems.at[CHUNKS + 2]),
    ]
    copies = []
    for c in range(CHUNKS):
        part = pl.ds(c * size, size)
        copies.append(pltpu.make_async_copy(weight_hbm.at[part], weight_ref.at[part], sems.at[c]))
    for copy in small + copies:
        copy.start()
    for copy in small:
        copy.wait()
    for m in range(MOM):
        mom_ref[BLK * m : BLK * (m + 1), :] = moment_ref[m].astype(jnp.float32)
    mom_ref[BLK * MOM :, :] = jnp.zeros((BLK * (16 - MOM), NZ), jnp.float32)
    tile, slab = tile_ref[...], slab_ref[...]
    step = slab - my_slab
    step = jnp.where(step == n_slabs - 1, -1, jnp.where(step == 1 - n_slabs, 1, step))
    plane = 1 + lax.shift_right_logical(tile, 7) + 2 * step
    row = lax.shift_right_logical(tile & 127, 1)
    used = iota((1, BLK), 1) < count_ref[0, 0]
    code = jnp.where(used, plane * NY + row + 1, 0).astype(jnp.float32)
    half = (tile & 1).astype(jnp.float32)
    both = jnp.where(iota((8, BLK), 0) == 0, code, half).astype(jnp.bfloat16)
    slot = iota((BLK, COLS), 0)
    slot = lax.shift_right_logical(slot, 1) + (slot & 1) * (BLK // 2)
    lane = iota((BLK, COLS), 1) - my_dom * 2 * BLK
    spread = jnp.where((lane == slot) | (lane == slot + BLK), 1.0, 0.0).astype(jnp.bfloat16)
    codes = jnp.dot(both, spread, preferred_element_type=jnp.float32).astype(jnp.bfloat16)
    out_ref[2 * BLK : ROWS, :] = jnp.concatenate([codes, codes], axis=0)
    low_half = iota((16, NZ), 1) < TC
    for b in range(0, BLK, GROUP):
        if b % size == 0:
            copies[b // size].wait()
        moms = [mom_ref[pl.ds(b + i, 16, stride=BLK), :] for i in range(GROUP)]
        mom = jnp.concatenate(moms, axis=0).astype(jnp.bfloat16)
        w = weight_ref[b : b + GROUP].reshape(GROUP * TC, NZ)
        term = lax.dot_general(mom, w, (((1,), (1,)), ((), ())), preferred_element_type=jnp.float32)
        for i in range(0, GROUP, 2):
            cols = slice(TC * i, TC * (i + 2))
            pair = jnp.where(low_half, term[16 * i : 16 * i + 16, cols], term[16 * i + 16 : 16 * i + 32, cols])
            term_ref[8 * (b + i) : 8 * (b + i) + 16, :] = pair
    for j in range(MOM // 2):
        even = term_ref[pl.ds(2 * j, BLK // 2, stride=16), :]
        odd = term_ref[pl.ds(2 * j + 1, BLK // 2, stride=16), :]
        rows = (
            jnp.where(low_half, even, pltpu.roll(odd, TC, 1)),
            jnp.where(low_half, pltpu.roll(even, TC, 1), odd),
        )
        term = jnp.concatenate(rows, axis=0)
        high = term.astype(jnp.bfloat16)
        low = (term - high.astype(jnp.float32)).astype(jnp.bfloat16)
        out_ref[0:BLK, NZ * j : NZ * (j + 1)] = high
        out_ref[BLK : 2 * BLK, NZ * j : NZ * (j + 1)] = low


def deposit(x_ref, top_row):
    codes = x_ref[2 * BLK : ROWS, :].astype(jnp.float32)
    for k in range(1, 8):
        codes += x_ref[ROWS * k + 2 * BLK : ROWS * (k + 1), :].astype(jnp.float32)
    code = codes[0:1, :KEPT].astype(jnp.int32) - 1
    half = codes[1:2, :KEPT].astype(jnp.int32)
    plane = lax.shift_right_arithmetic(code, 6)
    rel = (code & (NY - 1)) - top_row
    valid = (code >= 0) & (rel >= -HALO) & (rel < CHIP_ROWS + HALO)
    spot = (half * PLANES + plane) * WIN + jnp.where(rel < 0, rel + WIN, rel)
    spot = jnp.where(valid, spot, -1)
    chosen = jnp.where(iota((2 * PLANES * WIN, KEPT), 0) == spot, 1.0, 0.0).astype(jnp.bfloat16)
    terms = jnp.concatenate([x_ref[ROWS * k : ROWS * k + 2 * BLK, :] for k in range(8)], axis=0)
    return jnp.dot(chosen, terms, preferred_element_type=jnp.float32)


class Stencil:
    def __init__(self, top_row):
        self.lane = iota((WIN, NZ), 1)
        ring = iota((WIN, NZ), 0)
        at_row = top_row + jnp.where(ring < CHIP_ROWS + HALO, ring, ring - WIN)
        self.inside = (at_row >= 0) & (at_row < NY)

    def planes(self, cells, m):
        chunk = slice(NZ * (m // 2), NZ * (m // 2 + 1))
        out = []
        for q in range(PLANES):
            lower = cells[WIN * q : WIN * (q + 1), chunk]
            upper = cells[WIN * (PLANES + q) : WIN * (PLANES + q + 1), chunk]
            if m % 2 == 0:
                upper = pltpu.roll(upper, TC, 1)
            else:
                lower = pltpu.roll(lower, TC, 1)
            out.append(jnp.where(self.lane < TC, lower, upper))
        return out

    def flat(self, f):
        z = jnp.where(self.lane == 0, 0.0, pltpu.roll(f, 1, 1)) + jnp.where(
            self.lane == NZ - 1, 0.0, pltpu.roll(f, NZ - 1, 1)
        )
        y = pltpu.roll(f, 1, 0) + pltpu.roll(f, WIN - 1, 0)
        return keep_weight * f + diffusion * (y + z)

    def kept(self, f):
        return jnp.where(self.inside, f, 0.0)


def send_kernel(x_ref, early_ref, outer_ref, late_ref, part_ref):
    my_slab, my_dom = lax.axis_index("slab"), lax.axis_index("dom")
    core = lax.rem(my_dom, 2)
    top_row = (my_dom - core) * RY
    cells = deposit(x_ref, top_row)
    st = Stencil(top_row)

    def put(i, m, f):
        part_ref[i, m, 0] = f[0:RY]
        part_ref[i, m, 1] = f[RY : 2 * RY]

    for m in range(MOM):
        g = st.planes(cells, m)
        put(0, m, diffusion * diffusion * g[0])
        put(5, m, diffusion * diffusion * g[3])

        def near(g0, g1, g2, i_far, i_near):
            l0 = st.flat(g0)
            once0 = st.kept(l0 + diffusion * g1)
            once1 = st.kept(st.flat(g1) + diffusion * (g0 + g2))
            put(i_far, m, diffusion * (l0 + once0))
            put(i_near, m, st.flat(once0) + diffusion * (diffusion * g0 + once1))

        near(g[0], g[1], g[2], 1, 2)
        near(g[3], g[2], g[1], 4, 3)
    part_ref[6] = jnp.zeros((MOM, 2, RY, NZ), jnp.float32)

    sub = iota((RY, NZ), 0)
    for refs, odd_up in (((outer_ref,), 1), ((early_ref, late_ref), 0)):
        near_up = lax.rem(my_slab, 2) == odd_up
        far_up = lax.rem(lax.div(my_slab, 2), 2) == odd_up
        at = jnp.where(near_up, 3, 1)
        a = jnp.where(core == 1, at, jnp.where(far_up, 5, 6))
        b = jnp.where(core == 1, at + 1, jnp.where(far_up, 6, 0))
        tops = [jnp.zeros((RY, NZ), jnp.float32)] * 2
        for m in range(MOM):
            values = [part_ref[i, m, h] for h in range(2) for i in (a, b)]
            top = functools.reduce(jnp.maximum, [jnp.abs(v) for v in values])
            for k in (4, 2, 1):
                top = jnp.maximum(top, pltpu.roll(top, k, 0))
            top = jnp.floor(jnp.log2(jnp.maximum(top, 1e-30))) + 1.0
            factor = fixed_factor(top)
            tops[m // RY] = jnp.where(sub == m % RY, top, tops[m // RY])
            for k, v in enumerate(values):
                q = jnp.floor(v * factor + 0.5).astype(jnp.int32).astype(jnp.int16)
                for ref in refs:
                    ref[4 * m + k] = q
        for k in range(2):
            q = tops[k].astype(jnp.int32).astype(jnp.int16)
            for ref in refs:
                ref[4 * MOM + k] = q


def join_kernel(early_ref, outer_ref, late_ref, own_ref, mine_ref, other_ref):
    core = lax.rem(lax.axis_index("dom"), 2)
    refs = (early_ref, outer_ref, late_ref)
    tops = [[ref[4 * MOM + k].astype(jnp.float32) for k in range(2)] for ref in refs]
    for m in range(MOM):
        at = m % RY
        scales = [1.0 / fixed_factor(top[m // RY][at : at + 1]) for top in tops]
        for p in range(2):

            def arrived(h):
                parts = [ref[4 * m + 2 * h + p].astype(jnp.float32) * c for ref, c in zip(refs, scales)]
                return parts[0] + parts[1] + parts[2]

            other_ref[m, p] = arrived(1 - core)
            mine_ref[m, p] = own_ref[m, p] + arrived(core)


def own_kernel(x_ref, own_ref, part_ref):
    my_dom = lax.axis_index("dom")
    core = lax.rem(my_dom, 2)
    top_row = (my_dom - core) * RY
    cells = deposit(x_ref, top_row)
    st = Stencil(top_row)
    for m in range(MOM):
        g = st.planes(cells, m)
        flats = [st.flat(f) for f in g]
        once = [st.kept(flats[0] + diffusion * g[1])]
        once.append(st.kept(flats[1] + diffusion * (g[0] + g[2])))
        once.append(st.kept(flats[2] + diffusion * (g[1] + g[3])))
        once.append(st.kept(flats[3] + diffusion * g[2]))
        for p in range(2):
            f = st.flat(once[1 + p]) + diffusion * (once[p] + once[2 + p])
            part_ref[m, p, 0] = f[0:RY]
            part_ref[m, p, 1] = f[RY : 2 * RY]
    own_ref[...] = part_ref[:, :, core]


def swap_pairs(n_slabs, n_doms, odd_up, chosen):
    pairs = []
    for s in range(n_slabs):
        for d in range(n_doms):
            if not chosen(s):
                continue
            if d % 2 == 1:
                t = s + 1 if s % 2 == odd_up else s - 1
            else:
                t = s + 2 if (s // 2) % 2 == odd_up else s - 2
            pairs.append((d * n_slabs + s, d * n_slabs + t % n_slabs))
    return pairs


limited = pltpu.CompilerParams(vmem_limit_bytes=16 * 1024 * 1024)
alone = pltpu.CompilerParams(vmem_limit_bytes=60 * 1024 * 1024)
smem = pl.BlockSpec(memory_space=pltpu.SMEM)
hbm = pl.BlockSpec(memory_space=pltpu.HBM)
vmem = pl.BlockSpec(memory_space=pltpu.VMEM)


def make_terms(weights, moments, block_tile, block_slab, block_count):
    return pl.pallas_call(
        terms_kernel,
        out_shape=pltpu.VMEM((ROWS, COLS), jnp.bfloat16),
        in_specs=[smem] + [hbm] * 4,
        out_specs=vmem,
        scratch_shapes=[
            pltpu.VMEM((1, BLK), jnp.int32),
            pltpu.VMEM((1, BLK), jnp.int32),
            pltpu.VMEM((BLK, TC, NZ), jnp.bfloat16),
            pltpu.VMEM((MOM, BLK, NZ), jnp.bfloat16),
            pltpu.VMEM((8 * BLK, NZ), jnp.float32),
            pltpu.VMEM((16 * BLK, NZ), jnp.float32),
            pltpu.SemaphoreType.DMA((CHUNKS + 3,)),
        ],
        compiler_params=alone,
        name="terms",
    )(block_count, block_tile, block_slab, weights[0], moments[0].transpose(1, 0, 2))


def make_send(gathered):
    message = jax.ShapeDtypeStruct((4 * MOM + 2, RY, NZ), jnp.int16)
    return pl.pallas_call(
        send_kernel,
        out_shape=(message,) * 3,
        in_specs=[vmem],
        out_specs=(vmem,) * 3,
        scratch_shapes=[pltpu.VMEM((7, MOM, 2, RY, NZ), jnp.float32)],
        compiler_params=limited,
        name="send",
    )(gathered)


def make_own(gathered):
    return pl.pallas_call(
        own_kernel,
        out_shape=jax.ShapeDtypeStruct((MOM, 2, RY, NZ), jnp.float32),
        in_specs=[vmem],
        out_specs=vmem,
        scratch_shapes=[pltpu.VMEM((MOM, 2, 2, RY, NZ), jnp.float32)],
        cost_estimate=pl.CostEstimate(flops=400_000_000, bytes_accessed=8_000_000, transcendentals=0),
        compiler_params=limited,
        name="own",
    )(gathered)


def local(weights, moments, block_tile, block_slab, block_count):
    n_slabs = lax.axis_size("slab")
    n_doms = lax.axis_size("dom")
    x = make_terms(weights, moments, block_tile, block_slab, block_count)
    gathered = lax.all_gather(x, "dom", tiled=True)
    early, outer, late = make_send(gathered)
    both = ("dom", "slab")
    half = lambda low: lambda s: ((s // 4) % 8 < 4) == low
    early = lax.ppermute(early, both, swap_pairs(n_slabs, n_doms, 0, half(True)))
    outer = lax.ppermute(outer, both, swap_pairs(n_slabs, n_doms, 1, lambda s: True))
    late = lax.ppermute(late, both, swap_pairs(n_slabs, n_doms, 0, half(False)))
    own = make_own(gathered)
    early, outer, late, own = lax.optimization_barrier((early, outer, late, own))
    part = jax.ShapeDtypeStruct((MOM, 2, RY, NZ), jnp.float32)
    mine, other = pl.pallas_call(
        join_kernel,
        out_shape=(part, part),
        in_specs=[vmem] * 4,
        out_specs=(vmem, vmem),
        compiler_params=limited,
        name="join",
    )(early, outer, late, own)
    other = lax.ppermute(other, "dom", [(i, i ^ 1) for i in range(n_doms)])
    return mine + other


def solution(mesh):
    return jax.shard_map(
        local,
        mesh=mesh,
        in_specs=(
            P("slab", "dom", None, None),
            P("slab", "dom", None, None),
            P("slab", "dom"),
            P("slab", "dom"),
            P("slab", "dom"),
        ),
        out_specs=P(None, "slab", "dom", None),
        check_vma=False,
    )
```

```python
import functools

import jax
import jax.numpy as jnp
from jax import lax
from jax.experimental import pallas as pl
from jax.experimental.pallas import tpu as pltpu
from jax.sharding import PartitionSpec as P

MOM = 10
BLK = 32
TC = 64
NZ = 128
NY = 64
RY = 8
CHIP_ROWS = 2 * RY
HALO = 4
WIN = CHIP_ROWS + 2 * HALO
PLANES = 4
ROWS = 40
COLS = MOM * TC
KEPT = 8 * BLK
CHUNKS = 2
GROUP = 4
diffusion = 0.16
keep_weight = 1.0 - 6.0 * diffusion


def iota(shape, dim):
    return lax.broadcasted_iota(jnp.int32, shape, dim)


def fixed_factor(top):
    return jnp.exp2(14.9 - top)


def power(exponent):
    return jnp.exp2(exponent).astype(jnp.bfloat16).astype(jnp.float32)


def terms_kernel(
    count_ref, tile_hbm, slab_hbm, weight_hbm, moment_hbm, out_ref,
    tile_ref, slab_ref, weight_ref, moment_ref, term_ref, mom_ref, sems,
):
    my_slab, my_dom, n_slabs = lax.axis_index("slab"), lax.axis_index("dom"), lax.axis_size("slab")
    size = BLK // CHUNKS
    small = [
        pltpu.make_async_copy(moment_hbm, moment_ref, sems.at[CHUNKS]),
        pltpu.make_async_copy(tile_hbm, tile_ref, sems.at[CHUNKS + 1]),
        pltpu.make_async_copy(slab_hbm, slab_ref, sems.at[CHUNKS + 2]),
    ]
    copies = []
    for c in range(CHUNKS):
        part = pl.ds(c * size, size)
        copies.append(pltpu.make_async_copy(weight_hbm.at[part], weight_ref.at[part], sems.at[c]))
    for copy in small + copies:
        copy.start()
    for copy in small:
        copy.wait()
    for m in range(MOM):
        mom_ref[BLK * m : BLK * (m + 1), :] = moment_ref[m].astype(jnp.float32)
    mom_ref[BLK * MOM :, :] = jnp.zeros((BLK * (16 - MOM), NZ), jnp.float32)
    tile, slab = tile_ref[...], slab_ref[...]
    step = slab - my_slab
    step = jnp.where(step == n_slabs - 1, -1, jnp.where(step == 1 - n_slabs, 1, step))
    plane = 1 + lax.shift_right_logical(tile, 7) + 2 * step
    row = lax.shift_right_logical(tile & 127, 1)
    used = iota((1, BLK), 1) < count_ref[0, 0]
    code = jnp.where(used, plane * NY + row + 1, 0).astype(jnp.float32)
    half = (tile & 1).astype(jnp.float32)
    both = jnp.where(iota((8, BLK), 0) == 0, code, half).astype(jnp.bfloat16)
    slot = iota((BLK, COLS), 0)
    slot = lax.shift_right_logical(slot, 1) + (slot & 1) * (BLK // 2)
    lane = iota((BLK, COLS), 1) - my_dom * BLK
    spread = jnp.where(lane == slot, 1.0, 0.0).astype(jnp.bfloat16)
    codes = jnp.dot(both, spread, preferred_element_type=jnp.float32)
    low_half = iota((16, NZ), 1) < TC
    for b in range(0, BLK, GROUP):
        if b % size == 0:
            copies[b // size].wait()
        moms = [mom_ref[pl.ds(b + i, 16, stride=BLK), :] for i in range(GROUP)]
        mom = jnp.concatenate(moms, axis=0).astype(jnp.bfloat16)
        w = weight_ref[b : b + GROUP].reshape(GROUP * TC, NZ)
        term = lax.dot_general(mom, w, (((1,), (1,)), ((), ())), preferred_element_type=jnp.float32)
        for i in range(0, GROUP, 2):
            cols = slice(TC * i, TC * (i + 2))
            pair = jnp.where(low_half, term[16 * i : 16 * i + 16, cols], term[16 * i + 16 : 16 * i + 32, cols])
            term_ref[8 * (b + i) : 8 * (b + i) + 16, :] = pair
    terms = []
    for j in range(MOM // 2):
        even = term_ref[pl.ds(2 * j, BLK // 2, stride=16), :]
        odd = term_ref[pl.ds(2 * j + 1, BLK // 2, stride=16), :]
        rows = (
            jnp.where(low_half, even, pltpu.roll(odd, TC, 1)),
            jnp.where(low_half, pltpu.roll(even, TC, 1), odd),
        )
        terms.append(jnp.concatenate(rows, axis=0))
    top = functools.reduce(jnp.maximum, [jnp.abs(term) for term in terms])
    top = jnp.max(top, axis=1, keepdims=True)
    top = jnp.floor(jnp.log2(jnp.maximum(top, 1e-30))) + 1.0
    factor = power(15.0 - top)
    for j, term in enumerate(terms):
        q = jnp.clip(jnp.floor(term * factor + 0.5), -32767.0, 32767.0)
        out_ref[0:BLK, NZ * j : NZ * (j + 1)] = q.astype(jnp.int32).astype(jnp.int16)
    tops = jnp.sum(jnp.where(lane == iota((BLK, COLS), 0), top, 0.0), axis=0, keepdims=True)
    codes = jnp.where(iota((8, COLS), 0) == 2, tops, codes)
    out_ref[BLK:ROWS, :] = codes.astype(jnp.int32).astype(jnp.int16)


def deposit(x_ref, top_row):
    codes = functools.reduce(
        jnp.add, [x_ref[ROWS * k + BLK : ROWS * (k + 1), :KEPT].astype(jnp.int32) for k in range(8)]
    )
    code = codes[0:1, :] - 1
    half = codes[1:2, :]
    scale = power(codes[2:3, :].astype(jnp.float32) - 15.0)
    plane = lax.shift_right_arithmetic(code, 6)
    rel = (code & (NY - 1)) - top_row
    valid = (code >= 0) & (rel >= -HALO) & (rel < CHIP_ROWS + HALO)
    spot = (half * PLANES + plane) * WIN + jnp.where(rel < 0, rel + WIN, rel)
    spot = jnp.where(valid, spot, -1)
    chosen = jnp.where(iota((2 * PLANES * WIN, KEPT), 0) == spot, scale, 0.0)
    chosen = jnp.concatenate([256.0 * chosen, chosen], axis=1).astype(jnp.bfloat16)
    terms = [x_ref[ROWS * k : ROWS * k + BLK, :].astype(jnp.int32) for k in range(8)]
    high = [lax.shift_right_arithmetic(q, 8).astype(jnp.float32).astype(jnp.bfloat16) for q in terms]
    low = [(q & 255).astype(jnp.float32).astype(jnp.bfloat16) for q in terms]
    return jnp.dot(chosen, jnp.concatenate(high + low, axis=0), preferred_element_type=jnp.float32)


class Stencil:
    def __init__(self, top_row):
        self.lane = iota((WIN, NZ), 1)
        ring = iota((WIN, NZ), 0)
        at_row = top_row + jnp.where(ring < CHIP_ROWS + HALO, ring, ring - WIN)
        self.inside = (at_row >= 0) & (at_row < NY)

    def planes(self, cells, m):
        chunk = slice(NZ * (m // 2), NZ * (m // 2 + 1))
        out = []
        for q in range(PLANES):
            lower = cells[WIN * q : WIN * (q + 1), chunk]
            upper = cells[WIN * (PLANES + q) : WIN * (PLANES + q + 1), chunk]
            if m % 2 == 0:
                upper = pltpu.roll(upper, TC, 1)
            else:
                lower = pltpu.roll(lower, TC, 1)
            out.append(jnp.where(self.lane < TC, lower, upper))
        return out

    def flat(self, f):
        z = jnp.where(self.lane == 0, 0.0, pltpu.roll(f, 1, 1)) + jnp.where(
            self.lane == NZ - 1, 0.0, pltpu.roll(f, NZ - 1, 1)
        )
        y = pltpu.roll(f, 1, 0) + pltpu.roll(f, WIN - 1, 0)
        return keep_weight * f + diffusion * (y + z)

    def kept(self, f):
        return jnp.where(self.inside, f, 0.0)


def send_kernel(x_ref, early_ref, outer_ref, late_ref, part_ref):
    my_slab, my_dom = lax.axis_index("slab"), lax.axis_index("dom")
    core = lax.rem(my_dom, 2)
    top_row = (my_dom - core) * RY
    cells = deposit(x_ref, top_row)
    st = Stencil(top_row)

    def put(i, m, f):
        part_ref[i, m, 0] = f[0:RY]
        part_ref[i, m, 1] = f[RY : 2 * RY]

    for m in range(MOM):
        g = st.planes(cells, m)
        put(0, m, diffusion * diffusion * g[0])
        put(5, m, diffusion * diffusion * g[3])

        def near(g0, g1, g2, i_far, i_near):
            l0 = st.flat(g0)
            once0 = st.kept(l0 + diffusion * g1)
            once1 = st.kept(st.flat(g1) + diffusion * (g0 + g2))
            put(i_far, m, diffusion * (l0 + once0))
            put(i_near, m, st.flat(once0) + diffusion * (diffusion * g0 + once1))

        near(g[0], g[1], g[2], 1, 2)
        near(g[3], g[2], g[1], 4, 3)
    part_ref[6] = jnp.zeros((MOM, 2, RY, NZ), jnp.float32)

    sub = iota((RY, NZ), 0)
    for refs, odd_up in (((outer_ref,), 1), ((early_ref, late_ref), 0)):
        near_up = lax.rem(my_slab, 2) == odd_up
        far_up = lax.rem(lax.div(my_slab, 2), 2) == odd_up
        at = jnp.where(near_up, 3, 1)
        a = jnp.where(core == 1, at, jnp.where(far_up, 5, 6))
        b = jnp.where(core == 1, at + 1, jnp.where(far_up, 6, 0))
        tops = [jnp.zeros((RY, NZ), jnp.float32)] * 2
        for m in range(MOM):
            values = [part_ref[i, m, h] for h in range(2) for i in (a, b)]
            top = functools.reduce(jnp.maximum, [jnp.abs(v) for v in values])
            for k in (4, 2, 1):
                top = jnp.maximum(top, pltpu.roll(top, k, 0))
            top = jnp.floor(jnp.log2(jnp.maximum(top, 1e-30))) + 1.0
            factor = fixed_factor(top)
            tops[m // RY] = jnp.where(sub == m % RY, top, tops[m // RY])
            for k, v in enumerate(values):
                q = jnp.floor(v * factor + 0.5).astype(jnp.int32).astype(jnp.int16)
                for ref in refs:
                    ref[4 * m + k] = q
        for k in range(2):
            q = tops[k].astype(jnp.int32).astype(jnp.int16)
            for ref in refs:
                ref[4 * MOM + k] = q


def join_kernel(early_ref, outer_ref, late_ref, own_ref, mine_ref, other_ref):
    core = lax.rem(lax.axis_index("dom"), 2)
    refs = (early_ref, outer_ref, late_ref)
    tops = [[ref[4 * MOM + k].astype(jnp.float32) for k in range(2)] for ref in refs]
    for m in range(MOM):
        at = m % RY
        scales = [1.0 / fixed_factor(top[m // RY][at : at + 1]) for top in tops]
        for p in range(2):

            def arrived(h):
                parts = [ref[4 * m + 2 * h + p].astype(jnp.float32) * c for ref, c in zip(refs, scales)]
                return parts[0] + parts[1] + parts[2]

            other_ref[m, p] = arrived(1 - core)
            mine_ref[m, p] = own_ref[m, p] + arrived(core)


def own_kernel(x_ref, own_ref, part_ref):
    my_dom = lax.axis_index("dom")
    core = lax.rem(my_dom, 2)
    top_row = (my_dom - core) * RY
    cells = deposit(x_ref, top_row)
    st = Stencil(top_row)
    for m in range(MOM):
        g = st.planes(cells, m)
        flats = [st.flat(f) for f in g]
        once = [st.kept(flats[0] + diffusion * g[1])]
        once.append(st.kept(flats[1] + diffusion * (g[0] + g[2])))
        once.append(st.kept(flats[2] + diffusion * (g[1] + g[3])))
        once.append(st.kept(flats[3] + diffusion * g[2]))
        for p in range(2):
            f = st.flat(once[1 + p]) + diffusion * (once[p] + once[2 + p])
            part_ref[m, p, 0] = f[0:RY]
            part_ref[m, p, 1] = f[RY : 2 * RY]
    own_ref[...] = part_ref[:, :, core]


def swap_pairs(n_slabs, n_doms, odd_up, chosen):
    pairs = []
    for s in range(n_slabs):
        for d in range(n_doms):
            if not chosen(s):
                continue
            if d % 2 == 1:
                t = s + 1 if s % 2 == odd_up else s - 1
            else:
                t = s + 2 if (s // 2) % 2 == odd_up else s - 2
            pairs.append((d * n_slabs + s, d * n_slabs + t % n_slabs))
    return pairs


limited = pltpu.CompilerParams(vmem_limit_bytes=16 * 1024 * 1024)
alone = pltpu.CompilerParams(vmem_limit_bytes=60 * 1024 * 1024)
smem = pl.BlockSpec(memory_space=pltpu.SMEM)
hbm = pl.BlockSpec(memory_space=pltpu.HBM)
vmem = pl.BlockSpec(memory_space=pltpu.VMEM)


def make_terms(weights, moments, block_tile, block_slab, block_count):
    return pl.pallas_call(
        terms_kernel,
        out_shape=pltpu.VMEM((ROWS, COLS), jnp.int16),
        in_specs=[smem] + [hbm] * 4,
        out_specs=vmem,
        scratch_shapes=[
            pltpu.VMEM((1, BLK), jnp.int32),
            pltpu.VMEM((1, BLK), jnp.int32),
            pltpu.VMEM((BLK, TC, NZ), jnp.bfloat16),
            pltpu.VMEM((MOM, BLK, NZ), jnp.bfloat16),
            pltpu.VMEM((8 * BLK, NZ), jnp.float32),
            pltpu.VMEM((16 * BLK, NZ), jnp.float32),
            pltpu.SemaphoreType.DMA((CHUNKS + 3,)),
        ],
        compiler_params=alone,
        name="terms",
    )(block_count, block_tile, block_slab, weights[0], moments[0].transpose(1, 0, 2))


def make_send(gathered):
    message = jax.ShapeDtypeStruct((4 * MOM + 2, RY, NZ), jnp.int16)
    return pl.pallas_call(
        send_kernel,
        out_shape=(message,) * 3,
        in_specs=[vmem],
        out_specs=(vmem,) * 3,
        scratch_shapes=[pltpu.VMEM((7, MOM, 2, RY, NZ), jnp.float32)],
        compiler_params=limited,
        name="send",
    )(gathered)


def make_own(gathered):
    return pl.pallas_call(
        own_kernel,
        out_shape=jax.ShapeDtypeStruct((MOM, 2, RY, NZ), jnp.float32),
        in_specs=[vmem],
        out_specs=vmem,
        scratch_shapes=[pltpu.VMEM((MOM, 2, 2, RY, NZ), jnp.float32)],
        cost_estimate=pl.CostEstimate(flops=400_000_000, bytes_accessed=8_000_000, transcendentals=0),
        compiler_params=limited,
        name="own",
    )(gathered)


def local(weights, moments, block_tile, block_slab, block_count):
    n_slabs = lax.axis_size("slab")
    n_doms = lax.axis_size("dom")
    x = make_terms(weights, moments, block_tile, block_slab, block_count)
    gathered = lax.all_gather(x, "dom", tiled=True)
    early, outer, late = make_send(gathered)
    both = ("dom", "slab")
    half = lambda low: lambda s: ((s // 4) % 8 < 4) == low
    early = lax.ppermute(early, both, swap_pairs(n_slabs, n_doms, 0, half(True)))
    outer = lax.ppermute(outer, both, swap_pairs(n_slabs, n_doms, 1, lambda s: True))
    late = lax.ppermute(late, both, swap_pairs(n_slabs, n_doms, 0, half(False)))
    own = make_own(gathered)
    early, outer, late, own = lax.optimization_barrier((early, outer, late, own))
    part = jax.ShapeDtypeStruct((MOM, 2, RY, NZ), jnp.float32)
    mine, other = pl.pallas_call(
        join_kernel,
        out_shape=(part, part),
        in_specs=[vmem] * 4,
        out_specs=(vmem, vmem),
        compiler_params=limited,
        name="join",
    )(early, outer, late, own)
    other = lax.ppermute(other, "dom", [(i, i ^ 1) for i in range(n_doms)])
    return mine + other


def solution(mesh):
    return jax.shard_map(
        local,
        mesh=mesh,
        in_specs=(
            P("slab", "dom", None, None),
            P("slab", "dom", None, None),
            P("slab", "dom"),
            P("slab", "dom"),
            P("slab", "dom"),
        ),
        out_specs=P(None, "slab", "dom", None),
        check_vma=False,
    )
```

```python
import functools

import jax
import jax.numpy as jnp
from jax import lax
from jax.experimental import pallas as pl
from jax.experimental.pallas import tpu as pltpu
from jax.sharding import PartitionSpec as P

MOM = 10
BLK = 32
TC = 64
NZ = 128
NY = 64
RY = 8
CHIP_ROWS = 2 * RY
HALO = 4
WIN = CHIP_ROWS + 2 * HALO
PLANES = 4
ROWS = 40
COLS = MOM * TC
KEPT = 8 * BLK
CHUNKS = 2
GROUP = 4
diffusion = 0.16
keep_weight = 1.0 - 6.0 * diffusion


def iota(shape, dim):
    return lax.broadcasted_iota(jnp.int32, shape, dim)


def fixed_factor(top):
    return jnp.exp2(14.9 - top)


def power(exponent):
    return jnp.exp2(exponent).astype(jnp.bfloat16).astype(jnp.float32)


def terms_kernel(
    count_ref, tile_hbm, slab_hbm, weight_hbm, moment_hbm, out_ref,
    tile_ref, slab_ref, weight_ref, moment_ref, term_ref, mom_ref, sems,
):
    my_slab, my_dom, n_slabs = lax.axis_index("slab"), lax.axis_index("dom"), lax.axis_size("slab")
    size = BLK // CHUNKS
    small = [
        pltpu.make_async_copy(moment_hbm, moment_ref, sems.at[CHUNKS]),
        pltpu.make_async_copy(tile_hbm, tile_ref, sems.at[CHUNKS + 1]),
        pltpu.make_async_copy(slab_hbm, slab_ref, sems.at[CHUNKS + 2]),
    ]
    copies = []
    for c in range(CHUNKS):
        part = pl.ds(c * size, size)
        copies.append(pltpu.make_async_copy(weight_hbm.at[part], weight_ref.at[part], sems.at[c]))
    for copy in small + copies:
        copy.start()
    for copy in small:
        copy.wait()
    for m in range(MOM):
        mom_ref[BLK * m : BLK * (m + 1), :] = moment_ref[m].astype(jnp.float32)
    mom_ref[BLK * MOM :, :] = jnp.zeros((BLK * (16 - MOM), NZ), jnp.float32)
    tile, slab = tile_ref[...], slab_ref[...]
    step = slab - my_slab
    step = jnp.where(step == n_slabs - 1, -1, jnp.where(step == 1 - n_slabs, 1, step))
    plane = 1 + lax.shift_right_logical(tile, 7) + 2 * step
    row = lax.shift_right_logical(tile & 127, 1)
    used = iota((1, BLK), 1) < count_ref[0, 0]
    code = jnp.where(used, plane * NY + row + 1, 0).astype(jnp.float32)
    half = (tile & 1).astype(jnp.float32)
    both = jnp.where(iota((8, BLK), 0) == 0, code, half).astype(jnp.bfloat16)
    slot = iota((BLK, COLS), 0)
    slot = lax.shift_right_logical(slot, 1) + (slot & 1) * (BLK // 2)
    lane = iota((BLK, COLS), 1) - my_dom * BLK
    spread = jnp.where(lane == slot, 1.0, 0.0).astype(jnp.bfloat16)
    codes = jnp.dot(both, spread, preferred_element_type=jnp.float32)
    low_half = iota((16, NZ), 1) < TC
    for b in range(0, BLK, GROUP):
        if b % size == 0:
            copies[b // size].wait()
        moms = [mom_ref[pl.ds(b + i, 16, stride=BLK), :] for i in range(GROUP)]
        mom = jnp.concatenate(moms, axis=0).astype(jnp.bfloat16)
        w = weight_ref[b : b + GROUP].reshape(GROUP * TC, NZ)
        term = lax.dot_general(mom, w, (((1,), (1,)), ((), ())), preferred_element_type=jnp.float32)
        for i in range(0, GROUP, 2):
            cols = slice(TC * i, TC * (i + 2))
            pair = jnp.where(low_half, term[16 * i : 16 * i + 16, cols], term[16 * i + 16 : 16 * i + 32, cols])
            term_ref[8 * (b + i) : 8 * (b + i) + 16, :] = pair
    terms = []
    for j in range(MOM // 2):
        even = term_ref[pl.ds(2 * j, BLK // 2, stride=16), :]
        odd = term_ref[pl.ds(2 * j + 1, BLK // 2, stride=16), :]
        rows = (
            jnp.where(low_half, even, pltpu.roll(odd, TC, 1)),
            jnp.where(low_half, pltpu.roll(even, TC, 1), odd),
        )
        terms.append(jnp.concatenate(rows, axis=0))
    top = functools.reduce(jnp.maximum, [jnp.abs(term) for term in terms])
    top = jnp.max(top, axis=1, keepdims=True)
    top = jnp.floor(jnp.log2(jnp.maximum(top, 1e-33))) + 1.0
    factor = power(15.0 - top)
    for j, term in enumerate(terms):
        q = jnp.clip(jnp.floor(term * factor + 0.5), -32767.0, 32767.0)
        out_ref[0:BLK, NZ * j : NZ * (j + 1)] = q.astype(jnp.int32).astype(jnp.int16)
    tops = jnp.sum(jnp.where(lane == iota((BLK, COLS), 0), top, 0.0), axis=0, keepdims=True)
    codes = jnp.where(iota((8, COLS), 0) == 2, tops, codes)
    out_ref[BLK:ROWS, :] = codes.astype(jnp.int32).astype(jnp.int16)


def deposit(x_ref, top_row, flip):
    codes = functools.reduce(
        jnp.add, [x_ref[ROWS * k + BLK : ROWS * (k + 1), :KEPT].astype(jnp.int32) for k in range(8)]
    )
    code = codes[0:1, :] - 1
    half = codes[1:2, :]
    scale = power(codes[2:3, :].astype(jnp.float32) - 15.0)
    plane = lax.shift_right_arithmetic(code, 6)
    if flip is not False:
        plane = jnp.where(flip, PLANES - 1 - plane, plane)
    rel = (code & (NY - 1)) - top_row
    valid = (code >= 0) & (rel >= -HALO) & (rel < CHIP_ROWS + HALO)
    spot = (half * PLANES + plane) * WIN + jnp.where(rel < 0, rel + WIN, rel)
    spot = jnp.where(valid, spot, -1)
    chosen = jnp.where(iota((2 * PLANES * WIN, KEPT), 0) == spot, scale, 0.0)
    chosen = jnp.concatenate([256.0 * chosen, chosen], axis=1).astype(jnp.bfloat16)
    terms = [x_ref[ROWS * k : ROWS * k + BLK, :].astype(jnp.int32) for k in range(8)]
    high = [lax.shift_right_arithmetic(q, 8).astype(jnp.float32).astype(jnp.bfloat16) for q in terms]
    low = [(q & 255).astype(jnp.float32).astype(jnp.bfloat16) for q in terms]
    return jnp.dot(chosen, jnp.concatenate(high + low, axis=0), preferred_element_type=jnp.float32)


class Stencil:
    def __init__(self, top_row):
        self.lane = iota((WIN, NZ), 1)
        ring = iota((WIN, NZ), 0)
        at_row = top_row + jnp.where(ring < CHIP_ROWS + HALO, ring, ring - WIN)
        self.inside = (at_row >= 0) & (at_row < NY)

    def planes(self, cells, m):
        chunk = slice(NZ * (m // 2), NZ * (m // 2 + 1))
        out = []
        for q in range(PLANES):
            lower = cells[WIN * q : WIN * (q + 1), chunk]
            upper = cells[WIN * (PLANES + q) : WIN * (PLANES + q + 1), chunk]
            if m % 2 == 0:
                upper = pltpu.roll(upper, TC, 1)
            else:
                lower = pltpu.roll(lower, TC, 1)
            out.append(jnp.where(self.lane < TC, lower, upper))
        return out

    def flat(self, f):
        z = jnp.where(self.lane == 0, 0.0, pltpu.roll(f, 1, 1)) + jnp.where(
            self.lane == NZ - 1, 0.0, pltpu.roll(f, NZ - 1, 1)
        )
        y = pltpu.roll(f, 1, 0) + pltpu.roll(f, WIN - 1, 0)
        return keep_weight * f + diffusion * (y + z)

    def kept(self, f):
        return jnp.where(self.inside, f, 0.0)


def make_message(planes_of, st, core, far_up, near_up, ref, part_ref):
    for m in range(MOM):
        g0, g1, g2, g3 = planes_of(m)
        l0 = st.flat(g0)
        once0 = st.kept(l0 + diffusion * g1)
        once1 = st.kept(st.flat(g1) + diffusion * (g0 + g2))
        parts = (
            diffusion * diffusion * g0,
            diffusion * (l0 + once0),
            st.flat(once0) + diffusion * (diffusion * g0 + once1),
            diffusion * diffusion * g3,
        )
        for i, f in enumerate(parts):
            part_ref[i, m, 0] = f[0:RY]
            part_ref[i, m, 1] = f[RY : 2 * RY]
    part_ref[4] = jnp.zeros((MOM, 2, RY, NZ), jnp.float32)
    a = jnp.where(core == 1, jnp.where(near_up, 2, 1), jnp.where(far_up, jnp.where(near_up, 0, 3), 4))
    b = jnp.where(core == 1, jnp.where(near_up, 1, 2), jnp.where(far_up, 4, jnp.where(near_up, 3, 0)))
    sub = iota((RY, NZ), 0)
    tops = [jnp.zeros((RY, NZ), jnp.float32)] * 2
    for m in range(MOM):
        values = [part_ref[i, m, h] for h in range(2) for i in (a, b)]
        top = functools.reduce(jnp.maximum, [jnp.abs(v) for v in values])
        for k in (4, 2, 1):
            top = jnp.maximum(top, pltpu.roll(top, k, 0))
        top = jnp.floor(jnp.log2(jnp.maximum(top, 1e-33))) + 1.0
        factor = fixed_factor(top)
        tops[m // RY] = jnp.where(sub == m % RY, top, tops[m // RY])
        for k, v in enumerate(values):
            ref[4 * m + k] = jnp.floor(v * factor + 0.5).astype(jnp.int32).astype(jnp.int16)
    for k in range(2):
        ref[4 * MOM + k] = tops[k].astype(jnp.int32).astype(jnp.int16)


def where_am_i():
    my_slab, my_dom = lax.axis_index("slab"), lax.axis_index("dom")
    core = lax.rem(my_dom, 2)
    odd = lax.rem(my_slab, 2) == 1
    upper = lax.rem(lax.div(my_slab, 2), 2) == 1
    early = lax.rem(lax.div(my_slab, 4), 8) < 4
    return core, (my_dom - core) * RY, odd, upper, early


def send_kernel(x_ref, early_ref, outer_ref, part_ref):
    core, top_row, odd, upper, early = where_am_i()
    cells = deposit(x_ref, top_row, odd)
    st = Stencil(top_row)
    make_message(lambda m: st.planes(cells, m), st, core, upper, odd, outer_ref, part_ref)

    @pl.when(early)
    def _():
        inner = lambda m: st.planes(cells, m)[::-1]
        make_message(inner, st, core, jnp.logical_not(upper), jnp.logical_not(odd), early_ref, part_ref)


def late_kernel(x_ref, late_ref, part_ref):
    core, top_row, odd, upper, early = where_am_i()

    @pl.when(jnp.logical_not(early))
    def _():
        cells = deposit(x_ref, top_row, jnp.logical_not(odd))
        st = Stencil(top_row)
        planes = lambda m: st.planes(cells, m)
        make_message(planes, st, core, jnp.logical_not(upper), jnp.logical_not(odd), late_ref, part_ref)


def own_kernel(x_ref, own_ref, part_ref):
    core, top_row, _, _, _ = where_am_i()
    cells = deposit(x_ref, top_row, False)
    st = Stencil(top_row)
    for m in range(MOM):
        g = st.planes(cells, m)
        flats = [st.flat(f) for f in g]
        once = [st.kept(flats[0] + diffusion * g[1])]
        once.append(st.kept(flats[1] + diffusion * (g[0] + g[2])))
        once.append(st.kept(flats[2] + diffusion * (g[1] + g[3])))
        once.append(st.kept(flats[3] + diffusion * g[2]))
        for p in range(2):
            f = st.flat(once[1 + p]) + diffusion * (once[p] + once[2 + p])
            part_ref[m, p, 0] = f[0:RY]
            part_ref[m, p, 1] = f[RY : 2 * RY]
    own_ref[...] = part_ref[:, :, core]


def join_kernel(early_ref, outer_ref, late_ref, own_ref, mine_ref, other_ref):
    core = lax.rem(lax.axis_index("dom"), 2)
    refs = (early_ref, outer_ref, late_ref)
    tops = [[ref[4 * MOM + k].astype(jnp.float32) for k in range(2)] for ref in refs]
    for m in range(MOM):
        at = m % RY
        scales = [1.0 / fixed_factor(top[m // RY][at : at + 1]) for top in tops]
        for p in range(2):

            def arrived(h):
                parts = [ref[4 * m + 2 * h + p].astype(jnp.float32) * c for ref, c in zip(refs, scales)]
                return parts[0] + parts[1] + parts[2]

            other_ref[m, p] = arrived(1 - core)
            mine_ref[m, p] = own_ref[m, p] + arrived(core)


def swap_pairs(n_slabs, n_doms, odd_up, chosen):
    pairs = []
    for s in range(n_slabs):
        for d in range(n_doms):
            if not chosen(s):
                continue
            if d % 2 == 1:
                t = s + 1 if s % 2 == odd_up else s - 1
            else:
                t = s + 2 if (s // 2) % 2 == odd_up else s - 2
            pairs.append((d * n_slabs + s, d * n_slabs + t % n_slabs))
    return pairs


limited = pltpu.CompilerParams(vmem_limit_bytes=16 * 1024 * 1024)
alone = pltpu.CompilerParams(vmem_limit_bytes=60 * 1024 * 1024)
smem = pl.BlockSpec(memory_space=pltpu.SMEM)
hbm = pl.BlockSpec(memory_space=pltpu.HBM)
vmem = pl.BlockSpec(memory_space=pltpu.VMEM)


def make_terms(weights, moments, block_tile, block_slab, block_count):
    return pl.pallas_call(
        terms_kernel,
        out_shape=pltpu.VMEM((ROWS, COLS), jnp.int16),
        in_specs=[smem] + [hbm] * 4,
        out_specs=vmem,
        scratch_shapes=[
            pltpu.VMEM((1, BLK), jnp.int32),
            pltpu.VMEM((1, BLK), jnp.int32),
            pltpu.VMEM((BLK, TC, NZ), jnp.bfloat16),
            pltpu.VMEM((MOM, BLK, NZ), jnp.bfloat16),
            pltpu.VMEM((8 * BLK, NZ), jnp.float32),
            pltpu.VMEM((16 * BLK, NZ), jnp.float32),
            pltpu.SemaphoreType.DMA((CHUNKS + 3,)),
        ],
        compiler_params=alone,
        name="terms",
    )(block_count, block_tile, block_slab, weights[0], moments[0].transpose(1, 0, 2))


message = jax.ShapeDtypeStruct((4 * MOM + 2, RY, NZ), jnp.int16)
part = jax.ShapeDtypeStruct((MOM, 2, RY, NZ), jnp.float32)


def make_send(gathered):
    return pl.pallas_call(
        send_kernel,
        out_shape=(message, message),
        in_specs=[vmem],
        out_specs=(vmem, vmem),
        scratch_shapes=[pltpu.VMEM((5, MOM, 2, RY, NZ), jnp.float32)],
        compiler_params=limited,
        name="send",
    )(gathered)


def make_late(gathered):
    return pl.pallas_call(
        late_kernel,
        out_shape=message,
        in_specs=[vmem],
        out_specs=vmem,
        scratch_shapes=[pltpu.VMEM((5, MOM, 2, RY, NZ), jnp.float32)],
        compiler_params=limited,
        cost_estimate=pl.CostEstimate(flops=400_000_000, bytes_accessed=8_000_000, transcendentals=0),
        name="late",
    )(gathered)


def make_own(gathered):
    return pl.pallas_call(
        own_kernel,
        out_shape=part,
        in_specs=[vmem],
        out_specs=vmem,
        scratch_shapes=[pltpu.VMEM((MOM, 2, 2, RY, NZ), jnp.float32)],
        compiler_params=limited,
        cost_estimate=pl.CostEstimate(flops=400_000_000, bytes_accessed=8_000_000, transcendentals=0),
        name="own",
    )(gathered)


def local(weights, moments, block_tile, block_slab, block_count):
    n_slabs = lax.axis_size("slab")
    n_doms = lax.axis_size("dom")
    x = make_terms(weights, moments, block_tile, block_slab, block_count)
    gathered = lax.all_gather(x, "dom", tiled=True)
    early, outer = make_send(gathered)
    late = make_late(gathered)
    own = make_own(gathered)
    both = ("dom", "slab")
    half = lambda low: lambda s: ((s // 4) % 8 < 4) == low
    early = lax.ppermute(early, both, swap_pairs(n_slabs, n_doms, 0, half(True)))
    outer = lax.ppermute(outer, both, swap_pairs(n_slabs, n_doms, 1, lambda s: True))
    late = lax.ppermute(late, both, swap_pairs(n_slabs, n_doms, 0, half(False)))
    early, outer, late, own = lax.optimization_barrier((early, outer, late, own))
    mine, other = pl.pallas_call(
        join_kernel,
        out_shape=(part, part),
        in_specs=[vmem] * 4,
        out_specs=(vmem, vmem),
        compiler_params=limited,
        name="join",
    )(early, outer, late, own)
    other = lax.ppermute(other, "dom", [(i, i ^ 1) for i in range(n_doms)])
    return mine + other


def solution(mesh):
    return jax.shard_map(
        local,
        mesh=mesh,
        in_specs=(
            P("slab", "dom", None, None),
            P("slab", "dom", None, None),
            P("slab", "dom"),
            P("slab", "dom"),
            P("slab", "dom"),
        ),
        out_specs=P(None, "slab", "dom", None),
        check_vma=False,
    )
```

```python
import functools

import jax
import jax.numpy as jnp
from jax import lax
from jax.experimental import pallas as pl
from jax.experimental.pallas import tpu as pltpu
from jax.sharding import PartitionSpec as P

MOM = 10
BLK = 32
TC = 64
NZ = 128
NY = 64
RY = 8
CHIP_ROWS = 2 * RY
HALO = 4
WIN = CHIP_ROWS + 2 * HALO
PLANES = 4
ROWS = 40
COLS = MOM * TC
KEPT = 8 * BLK
CHUNKS = 1
GROUP = 4
diffusion = 0.16
keep_weight = 1.0 - 6.0 * diffusion


def iota(shape, dim):
    return lax.broadcasted_iota(jnp.int32, shape, dim)


def fixed_factor(top):
    return jnp.exp2(14.9 - top)


def power(exponent):
    return jnp.exp2(exponent).astype(jnp.bfloat16).astype(jnp.float32)


def terms_kernel(
    count_ref, tile_hbm, slab_hbm, weight_hbm, moment_hbm, out_ref,
    tile_ref, slab_ref, weight_ref, moment_ref, term_ref, mom_ref, sems,
):
    my_slab, my_dom, n_slabs = lax.axis_index("slab"), lax.axis_index("dom"), lax.axis_size("slab")
    size = BLK // CHUNKS
    small = [
        pltpu.make_async_copy(moment_hbm, moment_ref, sems.at[CHUNKS]),
        pltpu.make_async_copy(tile_hbm, tile_ref, sems.at[CHUNKS + 1]),
        pltpu.make_async_copy(slab_hbm, slab_ref, sems.at[CHUNKS + 2]),
    ]
    copies = []
    for c in range(CHUNKS):
        part = pl.ds(c * size, size)
        copies.append(pltpu.make_async_copy(weight_hbm.at[part], weight_ref.at[part], sems.at[c]))
    for copy in small + copies:
        copy.start()
    for copy in small:
        copy.wait()
    for m in range(MOM):
        mom_ref[BLK * m : BLK * (m + 1), :] = moment_ref[m].astype(jnp.float32)
    mom_ref[BLK * MOM :, :] = jnp.zeros((BLK * (16 - MOM), NZ), jnp.float32)
    tile, slab = tile_ref[...], slab_ref[...]
    step = slab - my_slab
    step = jnp.where(step == n_slabs - 1, -1, jnp.where(step == 1 - n_slabs, 1, step))
    plane = 1 + lax.shift_right_logical(tile, 7) + 2 * step
    row = lax.shift_right_logical(tile & 127, 1)
    used = iota((1, BLK), 1) < count_ref[0, 0]
    code = jnp.where(used, plane * NY + row + 1, 0).astype(jnp.float32)
    half = (tile & 1).astype(jnp.float32)
    both = jnp.where(iota((8, BLK), 0) == 0, code, half).astype(jnp.bfloat16)
    slot = iota((BLK, COLS), 0)
    slot = lax.shift_right_logical(slot, 1) + (slot & 1) * (BLK // 2)
    lane = iota((BLK, COLS), 1) - my_dom * BLK
    spread = jnp.where(lane == slot, 1.0, 0.0).astype(jnp.bfloat16)
    codes = jnp.dot(both, spread, preferred_element_type=jnp.float32)
    low_half = iota((16, NZ), 1) < TC
    for b in range(0, BLK, GROUP):
        if b % size == 0:
            copies[b // size].wait()
        moms = [mom_ref[pl.ds(b + i, 16, stride=BLK), :] for i in range(GROUP)]
        mom = jnp.concatenate(moms, axis=0).astype(jnp.bfloat16)
        w = weight_ref[b : b + GROUP].reshape(GROUP * TC, NZ)
        term = lax.dot_general(mom, w, (((1,), (1,)), ((), ())), preferred_element_type=jnp.float32)
        for i in range(0, GROUP, 2):
            cols = slice(TC * i, TC * (i + 2))
            pair = jnp.where(low_half, term[16 * i : 16 * i + 16, cols], term[16 * i + 16 : 16 * i + 32, cols])
            term_ref[8 * (b + i) : 8 * (b + i) + 16, :] = pair
    terms = []
    for j in range(MOM // 2):
        even = term_ref[pl.ds(2 * j, BLK // 2, stride=16), :]
        odd = term_ref[pl.ds(2 * j + 1, BLK // 2, stride=16), :]
        rows = (
            jnp.where(low_half, even, pltpu.roll(odd, TC, 1)),
            jnp.where(low_half, pltpu.roll(even, TC, 1), odd),
        )
        terms.append(jnp.concatenate(rows, axis=0))
    top = functools.reduce(jnp.maximum, [jnp.abs(term) for term in terms])
    top = jnp.max(top, axis=1, keepdims=True)
    top = jnp.floor(jnp.log2(jnp.maximum(top, 1e-33))) + 1.0
    factor = power(15.0 - top)
    for j, term in enumerate(terms):
        q = jnp.clip(jnp.floor(term * factor + 0.5), -32767.0, 32767.0)
        out_ref[0:BLK, NZ * j : NZ * (j + 1)] = q.astype(jnp.int32).astype(jnp.int16)
    tops = jnp.sum(jnp.where(lane == iota((BLK, COLS), 0), top, 0.0), axis=0, keepdims=True)
    codes = jnp.where(iota((8, COLS), 0) == 2, tops, codes)
    out_ref[BLK:ROWS, :] = codes.astype(jnp.int32).astype(jnp.int16)


def gathered_codes(x_ref):
    codes = functools.reduce(
        jnp.add, [x_ref[ROWS * k + BLK : ROWS * (k + 1), :KEPT].astype(jnp.int32) for k in range(8)]
    )
    code = codes[0:1, :] - 1
    scale = power(codes[2:3, :].astype(jnp.float32) - 15.0)
    return code, lax.shift_right_arithmetic(code, 6), code & (NY - 1), codes[1:2, :], scale


def gather_cells(x_ref, spot, scale, count):
    chosen = jnp.where(iota((count, KEPT), 0) == spot, scale, 0.0)
    chosen = jnp.concatenate([256.0 * chosen, chosen], axis=1).astype(jnp.bfloat16)
    terms = [x_ref[ROWS * k : ROWS * k + BLK, :].astype(jnp.int32) for k in range(8)]
    high = [lax.shift_right_arithmetic(q, 8).astype(jnp.float32).astype(jnp.bfloat16) for q in terms]
    low = [(q & 255).astype(jnp.float32).astype(jnp.bfloat16) for q in terms]
    return jnp.dot(chosen, jnp.concatenate(high + low, axis=0), preferred_element_type=jnp.float32)


def deposit(x_ref, top_row, flip):
    code, plane, row, half, scale = gathered_codes(x_ref)
    if flip is not False:
        plane = jnp.where(flip, PLANES - 1 - plane, plane)
    rel = row - top_row
    valid = (code >= 0) & (rel >= -HALO) & (rel < CHIP_ROWS + HALO)
    spot = (half * PLANES + plane) * WIN + jnp.where(rel < 0, rel + WIN, rel)
    return gather_cells(x_ref, jnp.where(valid, spot, -1), scale, 2 * PLANES * WIN)


class Stencil:
    def __init__(self, top_row):
        self.lane = iota((WIN, NZ), 1)
        ring = iota((WIN, NZ), 0)
        at_row = top_row + jnp.where(ring < CHIP_ROWS + HALO, ring, ring - WIN)
        self.inside = (at_row >= 0) & (at_row < NY)

    def planes(self, cells, m):
        chunk = slice(NZ * (m // 2), NZ * (m // 2 + 1))
        out = []
        for q in range(PLANES):
            lower = cells[WIN * q : WIN * (q + 1), chunk]
            upper = cells[WIN * (PLANES + q) : WIN * (PLANES + q + 1), chunk]
            if m % 2 == 0:
                upper = pltpu.roll(upper, TC, 1)
            else:
                lower = pltpu.roll(lower, TC, 1)
            out.append(jnp.where(self.lane < TC, lower, upper))
        return out

    def flat(self, f):
        z = jnp.where(self.lane == 0, 0.0, pltpu.roll(f, 1, 1)) + jnp.where(
            self.lane == NZ - 1, 0.0, pltpu.roll(f, NZ - 1, 1)
        )
        y = pltpu.roll(f, 1, 0) + pltpu.roll(f, WIN - 1, 0)
        return keep_weight * f + diffusion * (y + z)

    def kept(self, f):
        return jnp.where(self.inside, f, 0.0)


def quantize(values_of, ref):
    sub = iota((RY, NZ), 0)
    tops = [jnp.zeros((RY, NZ), jnp.float32)] * 2
    for m in range(MOM):
        values = values_of(m)
        top = functools.reduce(jnp.maximum, [jnp.abs(v) for v in values])
        for k in (4, 2, 1):
            top = jnp.maximum(top, pltpu.roll(top, k, 0))
        top = jnp.floor(jnp.log2(jnp.maximum(top, 1e-33))) + 1.0
        factor = fixed_factor(top)
        tops[m // RY] = jnp.where(sub == m % RY, top, tops[m // RY])
        for k, v in enumerate(values):
            ref[4 * m + k] = jnp.floor(v * factor + 0.5).astype(jnp.int32).astype(jnp.int16)
    for k in range(2):
        ref[4 * MOM + k] = tops[k].astype(jnp.int32).astype(jnp.int16)


def make_message(x_ref, core, top_row, far_up, near_up, ref, active):
    @pl.when(active & (core == 1))
    def _():
        cells = deposit(x_ref, top_row, near_up)
        st = Stencil(top_row)

        def values_of(m):
            g0, g1, g2, _ = st.planes(cells, m)
            l0 = st.flat(g0)
            once0 = st.kept(l0 + diffusion * g1)
            once1 = st.kept(st.flat(g1) + diffusion * (g0 + g2))
            outer = diffusion * (l0 + once0)
            inner = st.flat(once0) + diffusion * (diffusion * g0 + once1)
            first = jnp.where(near_up, inner, outer)
            second = jnp.where(near_up, outer, inner)
            return [f[RY * h : RY * (h + 1)] for h in range(2) for f in (first, second)]

        quantize(values_of, ref)

    @pl.when(active & (core == 0))
    def _():
        code, plane, row, half, scale = gathered_codes(x_ref)
        rel = row - top_row
        wanted = jnp.where(far_up, PLANES - 1, 0)
        valid = (code >= 0) & (plane == wanted) & (rel >= 0) & (rel < CHIP_ROWS)
        spot = jnp.where(valid, half * CHIP_ROWS + rel, -1)
        cells = gather_cells(x_ref, spot, scale, 2 * CHIP_ROWS)
        lane = iota((CHIP_ROWS, NZ), 1)

        def values_of(m):
            chunk = slice(NZ * (m // 2), NZ * (m // 2 + 1))
            lower, upper = cells[:CHIP_ROWS, chunk], cells[CHIP_ROWS:, chunk]
            if m % 2 == 0:
                upper = pltpu.roll(upper, TC, 1)
            else:
                lower = pltpu.roll(lower, TC, 1)
            f = diffusion * diffusion * jnp.where(lane < TC, lower, upper)
            pair = (jnp.where(far_up, f, 0.0), jnp.where(far_up, 0.0, f))
            return [g[RY * h : RY * (h + 1)] for h in range(2) for g in pair]

        quantize(values_of, ref)


def where_am_i():
    my_slab, my_dom = lax.axis_index("slab"), lax.axis_index("dom")
    core = lax.rem(my_dom, 2)
    odd = lax.rem(my_slab, 2) == 1
    upper = lax.rem(lax.div(my_slab, 2), 2) == 1
    early = lax.rem(lax.div(my_slab, 4), 8) < 4
    return core, (my_dom - core) * RY, odd, upper, early


def send_kernel(x_ref, early_ref, outer_ref):
    core, top_row, odd, upper, early = where_am_i()
    make_message(x_ref, core, top_row, upper, odd, outer_ref, True)
    make_message(x_ref, core, top_row, jnp.logical_not(upper), jnp.logical_not(odd), early_ref, early)


def late_kernel(x_ref, late_ref):
    core, top_row, odd, upper, early = where_am_i()
    late = jnp.logical_not(early)
    make_message(x_ref, core, top_row, jnp.logical_not(upper), jnp.logical_not(odd), late_ref, late)


def own_kernel(x_ref, own_ref, part_ref):
    core, top_row, _, _, _ = where_am_i()
    cells = deposit(x_ref, top_row, False)
    st = Stencil(top_row)
    for m in range(MOM):
        g = st.planes(cells, m)
        flats = [st.flat(f) for f in g]
        once = [st.kept(flats[0] + diffusion * g[1])]
        once.append(st.kept(flats[1] + diffusion * (g[0] + g[2])))
        once.append(st.kept(flats[2] + diffusion * (g[1] + g[3])))
        once.append(st.kept(flats[3] + diffusion * g[2]))
        for p in range(2):
            f = st.flat(once[1 + p]) + diffusion * (once[p] + once[2 + p])
            part_ref[m, p, 0] = f[0:RY]
            part_ref[m, p, 1] = f[RY : 2 * RY]
    own_ref[...] = part_ref[:, :, core]


def join_kernel(early_ref, outer_ref, late_ref, own_ref, mine_ref, other_ref):
    core = lax.rem(lax.axis_index("dom"), 2)
    refs = (early_ref, outer_ref, late_ref)
    tops = [[ref[4 * MOM + k].astype(jnp.float32) for k in range(2)] for ref in refs]
    for m in range(MOM):
        at = m % RY
        scales = [1.0 / fixed_factor(top[m // RY][at : at + 1]) for top in tops]
        for p in range(2):

            def arrived(h):
                parts = [ref[4 * m + 2 * h + p].astype(jnp.float32) * c for ref, c in zip(refs, scales)]
                return parts[0] + parts[1] + parts[2]

            other_ref[m, p] = arrived(1 - core)
            mine_ref[m, p] = own_ref[m, p] + arrived(core)


def swap_pairs(n_slabs, n_doms, odd_up, chosen):
    pairs = []
    for s in range(n_slabs):
        for d in range(n_doms):
            if not chosen(s):
                continue
            if d % 2 == 1:
                t = s + 1 if s % 2 == odd_up else s - 1
            else:
                t = s + 2 if (s // 2) % 2 == odd_up else s - 2
            pairs.append((d * n_slabs + s, d * n_slabs + t % n_slabs))
    return pairs


limited = pltpu.CompilerParams(vmem_limit_bytes=16 * 1024 * 1024)
alone = pltpu.CompilerParams(vmem_limit_bytes=60 * 1024 * 1024)
smem = pl.BlockSpec(memory_space=pltpu.SMEM)
hbm = pl.BlockSpec(memory_space=pltpu.HBM)
vmem = pl.BlockSpec(memory_space=pltpu.VMEM)


def make_terms(weights, moments, block_tile, block_slab, block_count):
    return pl.pallas_call(
        terms_kernel,
        out_shape=pltpu.VMEM((ROWS, COLS), jnp.int16),
        in_specs=[smem] + [hbm] * 4,
        out_specs=vmem,
        scratch_shapes=[
            pltpu.VMEM((1, BLK), jnp.int32),
            pltpu.VMEM((1, BLK), jnp.int32),
            pltpu.VMEM((BLK, TC, NZ), jnp.bfloat16),
            pltpu.VMEM((MOM, BLK, NZ), jnp.bfloat16),
            pltpu.VMEM((8 * BLK, NZ), jnp.float32),
            pltpu.VMEM((16 * BLK, NZ), jnp.float32),
            pltpu.SemaphoreType.DMA((CHUNKS + 3,)),
        ],
        compiler_params=alone,
        name="terms",
    )(block_count, block_tile, block_slab, weights[0], moments[0].transpose(1, 0, 2))


message = jax.ShapeDtypeStruct((4 * MOM + 2, RY, NZ), jnp.int16)
part = jax.ShapeDtypeStruct((MOM, 2, RY, NZ), jnp.float32)


def make_send(gathered):
    return pl.pallas_call(
        send_kernel,
        out_shape=(message, message),
        in_specs=[vmem],
        out_specs=(vmem, vmem),
        compiler_params=limited,
        name="send",
    )(gathered)


def make_late(gathered):
    return pl.pallas_call(
        late_kernel,
        out_shape=message,
        in_specs=[vmem],
        out_specs=vmem,
        compiler_params=limited,
        cost_estimate=pl.CostEstimate(flops=400_000_000, bytes_accessed=8_000_000, transcendentals=0),
        name="late",
    )(gathered)


def make_own(gathered):
    return pl.pallas_call(
        own_kernel,
        out_shape=part,
        in_specs=[vmem],
        out_specs=vmem,
        scratch_shapes=[pltpu.VMEM((MOM, 2, 2, RY, NZ), jnp.float32)],
        compiler_params=limited,
        cost_estimate=pl.CostEstimate(flops=400_000_000, bytes_accessed=8_000_000, transcendentals=0),
        name="own",
    )(gathered)


def local(weights, moments, block_tile, block_slab, block_count):
    n_slabs = lax.axis_size("slab")
    n_doms = lax.axis_size("dom")
    x = make_terms(weights, moments, block_tile, block_slab, block_count)
    gathered = lax.all_gather(x, "dom", tiled=True)
    early, outer = make_send(gathered)
    late = make_late(gathered)
    own = make_own(gathered)
    both = ("dom", "slab")
    half = lambda low: lambda s: ((s // 4) % 8 < 4) == low
    early = lax.ppermute(early, both, swap_pairs(n_slabs, n_doms, 0, half(True)))
    outer = lax.ppermute(outer, both, swap_pairs(n_slabs, n_doms, 1, lambda s: True))
    late = lax.ppermute(late, both, swap_pairs(n_slabs, n_doms, 0, half(False)))
    early, outer, late, own = lax.optimization_barrier((early, outer, late, own))
    mine, other = pl.pallas_call(
        join_kernel,
        out_shape=(part, part),
        in_specs=[vmem] * 4,
        out_specs=(vmem, vmem),
        compiler_params=limited,
        name="join",
    )(early, outer, late, own)
    other = lax.ppermute(other, "dom", [(i, i ^ 1) for i in range(n_doms)])
    return mine + other


def solution(mesh):
    return jax.shard_map(
        local,
        mesh=mesh,
        in_specs=(
            P("slab", "dom", None, None),
            P("slab", "dom", None, None),
            P("slab", "dom"),
            P("slab", "dom"),
            P("slab", "dom"),
        ),
        out_specs=P(None, "slab", "dom", None),
        check_vma=False,
    )
```

```python
import functools

import jax
import jax.numpy as jnp
from jax import lax
from jax.experimental import pallas as pl
from jax.experimental.pallas import tpu as pltpu
from jax.sharding import PartitionSpec as P

MOM = 10
BLK = 32
TC = 64
NZ = 128
NY = 64
RY = 8
CHIP_ROWS = 2 * RY
HALO = 4
WIN = CHIP_ROWS + 2 * HALO
PLANES = 4
ROWS = 40
COLS = MOM * TC
KEPT = 8 * BLK
CHUNKS = 1
GROUP = 4
diffusion = 0.16
keep_weight = 1.0 - 6.0 * diffusion


def iota(shape, dim):
    return lax.broadcasted_iota(jnp.int32, shape, dim)


def fixed_factor(top):
    return jnp.exp2(14.9 - top)


def power(exponent):
    return jnp.exp2(exponent).astype(jnp.bfloat16).astype(jnp.float32)


def terms_kernel(
    count_ref, tile_hbm, slab_hbm, weight_hbm, moment_hbm, out_ref,
    tile_ref, slab_ref, weight_ref, moment_ref, term_ref, mom_ref, sems,
):
    my_slab, my_dom, n_slabs = lax.axis_index("slab"), lax.axis_index("dom"), lax.axis_size("slab")
    size = BLK // CHUNKS
    small = [
        pltpu.make_async_copy(moment_hbm, moment_ref, sems.at[CHUNKS]),
        pltpu.make_async_copy(tile_hbm, tile_ref, sems.at[CHUNKS + 1]),
        pltpu.make_async_copy(slab_hbm, slab_ref, sems.at[CHUNKS + 2]),
    ]
    copies = []
    for c in range(CHUNKS):
        part = pl.ds(c * size, size)
        copies.append(pltpu.make_async_copy(weight_hbm.at[part], weight_ref.at[part], sems.at[c]))
    for copy in small + copies:
        copy.start()
    for copy in small:
        copy.wait()
    for m in range(MOM):
        mom_ref[BLK * m : BLK * (m + 1), :] = moment_ref[m].astype(jnp.float32)
    mom_ref[BLK * MOM :, :] = jnp.zeros((BLK * (16 - MOM), NZ), jnp.float32)
    tile, slab = tile_ref[...], slab_ref[...]
    step = slab - my_slab
    step = jnp.where(step == n_slabs - 1, -1, jnp.where(step == 1 - n_slabs, 1, step))
    plane = 1 + lax.shift_right_logical(tile, 7) + 2 * step
    row = lax.shift_right_logical(tile & 127, 1)
    used = iota((1, BLK), 1) < count_ref[0, 0]
    code = jnp.where(used, plane * NY + row + 1, 0).astype(jnp.float32)
    half = (tile & 1).astype(jnp.float32)
    both = jnp.where(iota((8, BLK), 0) == 0, code, half).astype(jnp.bfloat16)
    slot = iota((BLK, COLS), 0)
    slot = lax.shift_right_logical(slot, 1) + (slot & 1) * (BLK // 2)
    lane = iota((BLK, COLS), 1) - my_dom * BLK
    spread = jnp.where(lane == slot, 1.0, 0.0).astype(jnp.bfloat16)
    codes = jnp.dot(both, spread, preferred_element_type=jnp.float32)
    low_half = iota((16, NZ), 1) < TC
    for b in range(0, BLK, GROUP):
        if b % size == 0:
            copies[b // size].wait()
        moms = [mom_ref[pl.ds(b + i, 16, stride=BLK), :] for i in range(GROUP)]
        mom = jnp.concatenate(moms, axis=0).astype(jnp.bfloat16)
        w = weight_ref[b : b + GROUP].reshape(GROUP * TC, NZ)
        term = lax.dot_general(mom, w, (((1,), (1,)), ((), ())), preferred_element_type=jnp.float32)
        for i in range(0, GROUP, 2):
            cols = slice(TC * i, TC * (i + 2))
            pair = jnp.where(low_half, term[16 * i : 16 * i + 16, cols], term[16 * i + 16 : 16 * i + 32, cols])
            term_ref[8 * (b + i) : 8 * (b + i) + 16, :] = pair
    terms = []
    for j in range(MOM // 2):
        even = term_ref[pl.ds(2 * j, BLK // 2, stride=16), :]
        odd = term_ref[pl.ds(2 * j + 1, BLK // 2, stride=16), :]
        rows = (
            jnp.where(low_half, even, pltpu.roll(odd, TC, 1)),
            jnp.where(low_half, pltpu.roll(even, TC, 1), odd),
        )
        terms.append(jnp.concatenate(rows, axis=0))
    top = functools.reduce(jnp.maximum, [jnp.abs(term) for term in terms])
    top = jnp.max(top, axis=1, keepdims=True)
    top = jnp.floor(jnp.log2(jnp.maximum(top, 1e-33))) + 1.0
    factor = power(15.0 - top)
    for j, term in enumerate(terms):
        q = jnp.clip(jnp.floor(term * factor + 0.5), -32767.0, 32767.0)
        out_ref[0:BLK, NZ * j : NZ * (j + 1)] = q.astype(jnp.int32).astype(jnp.int16)
    tops = jnp.sum(jnp.where(lane == iota((BLK, COLS), 0), top, 0.0), axis=0, keepdims=True)
    codes = jnp.where(iota((8, COLS), 0) == 2, tops, codes)
    out_ref[BLK:ROWS, :] = codes.astype(jnp.int32).astype(jnp.int16)


def gathered_codes(x_ref):
    codes = functools.reduce(
        jnp.add, [x_ref[ROWS * k + BLK : ROWS * (k + 1), :KEPT].astype(jnp.int32) for k in range(8)]
    )
    code = codes[0:1, :] - 1
    scale = power(codes[2:3, :].astype(jnp.float32) - 15.0)
    return code, lax.shift_right_arithmetic(code, 6), code & (NY - 1), codes[1:2, :], scale


def gather_cells(x_ref, spot, scale, count):
    chosen = jnp.where(iota((count, KEPT), 0) == spot, scale, 0.0)
    chosen = jnp.concatenate([256.0 * chosen, chosen], axis=1).astype(jnp.bfloat16)
    terms = [x_ref[ROWS * k : ROWS * k + BLK, :].astype(jnp.int32) for k in range(8)]
    high = [lax.shift_right_arithmetic(q, 8).astype(jnp.float32).astype(jnp.bfloat16) for q in terms]
    low = [(q & 255).astype(jnp.float32).astype(jnp.bfloat16) for q in terms]
    return jnp.dot(chosen, jnp.concatenate(high + low, axis=0), preferred_element_type=jnp.float32)


def deposit(x_ref, top_row, flip, planes=PLANES):
    code, plane, row, half, scale = gathered_codes(x_ref)
    if flip is not False:
        plane = jnp.where(flip, PLANES - 1 - plane, plane)
    rel = row - top_row
    valid = (code >= 0) & (plane < planes) & (rel >= -HALO) & (rel < CHIP_ROWS + HALO)
    spot = (half * planes + plane) * WIN + jnp.where(rel < 0, rel + WIN, rel)
    return gather_cells(x_ref, jnp.where(valid, spot, -1), scale, 2 * planes * WIN)


class Stencil:
    def __init__(self, top_row):
        self.lane = iota((WIN, NZ), 1)
        ring = iota((WIN, NZ), 0)
        at_row = top_row + jnp.where(ring < CHIP_ROWS + HALO, ring, ring - WIN)
        self.inside = (at_row >= 0) & (at_row < NY)

    def planes(self, cells, m, count=PLANES):
        chunk = slice(NZ * (m // 2), NZ * (m // 2 + 1))
        out = []
        for q in range(count):
            lower = cells[WIN * q : WIN * (q + 1), chunk]
            upper = cells[WIN * (count + q) : WIN * (count + q + 1), chunk]
            if m % 2 == 0:
                upper = pltpu.roll(upper, TC, 1)
            else:
                lower = pltpu.roll(lower, TC, 1)
            out.append(jnp.where(self.lane < TC, lower, upper))
        return out

    def flat(self, f):
        z = jnp.where(self.lane == 0, 0.0, pltpu.roll(f, 1, 1)) + jnp.where(
            self.lane == NZ - 1, 0.0, pltpu.roll(f, NZ - 1, 1)
        )
        y = pltpu.roll(f, 1, 0) + pltpu.roll(f, WIN - 1, 0)
        return keep_weight * f + diffusion * (y + z)

    def kept(self, f):
        return jnp.where(self.inside, f, 0.0)


def quantize(values_of, ref):
    sub = iota((RY, NZ), 0)
    tops = [jnp.zeros((RY, NZ), jnp.float32)] * 2
    for m in range(MOM):
        values = values_of(m)
        top = functools.reduce(jnp.maximum, [jnp.abs(v) for v in values])
        for k in (4, 2, 1):
            top = jnp.maximum(top, pltpu.roll(top, k, 0))
        top = jnp.floor(jnp.log2(jnp.maximum(top, 1e-33))) + 1.0
        factor = fixed_factor(top)
        tops[m // RY] = jnp.where(sub == m % RY, top, tops[m // RY])
        for k, v in enumerate(values):
            ref[4 * m + k] = jnp.floor(v * factor + 0.5).astype(jnp.int32).astype(jnp.int16)
    for k in range(2):
        ref[4 * MOM + k] = tops[k].astype(jnp.int32).astype(jnp.int16)


def make_message(x_ref, core, top_row, far_up, near_up, ref, active):
    @pl.when(active & (core == 1))
    def _():
        cells = deposit(x_ref, top_row, near_up, 3)
        st = Stencil(top_row)

        def values_of(m):
            g0, g1, g2 = st.planes(cells, m, 3)
            l0 = st.flat(g0)
            once0 = st.kept(l0 + diffusion * g1)
            once1 = st.kept(st.flat(g1) + diffusion * (g0 + g2))
            outer = diffusion * (l0 + once0)
            inner = st.flat(once0) + diffusion * (diffusion * g0 + once1)
            first = jnp.where(near_up, inner, outer)
            second = jnp.where(near_up, outer, inner)
            return [f[RY * h : RY * (h + 1)] for h in range(2) for f in (first, second)]

        quantize(values_of, ref)

    @pl.when(active & (core == 0))
    def _():
        code, plane, row, half, scale = gathered_codes(x_ref)
        rel = row - top_row
        wanted = jnp.where(far_up, PLANES - 1, 0)
        valid = (code >= 0) & (plane == wanted) & (rel >= 0) & (rel < CHIP_ROWS)
        spot = jnp.where(valid, half * CHIP_ROWS + rel, -1)
        cells = gather_cells(x_ref, spot, scale, 2 * CHIP_ROWS)
        lane = iota((CHIP_ROWS, NZ), 1)

        def values_of(m):
            chunk = slice(NZ * (m // 2), NZ * (m // 2 + 1))
            lower, upper = cells[:CHIP_ROWS, chunk], cells[CHIP_ROWS:, chunk]
            if m % 2 == 0:
                upper = pltpu.roll(upper, TC, 1)
            else:
                lower = pltpu.roll(lower, TC, 1)
            f = diffusion * diffusion * jnp.where(lane < TC, lower, upper)
            pair = (jnp.where(far_up, f, 0.0), jnp.where(far_up, 0.0, f))
            return [g[RY * h : RY * (h + 1)] for h in range(2) for g in pair]

        quantize(values_of, ref)


def where_am_i():
    my_slab, my_dom = lax.axis_index("slab"), lax.axis_index("dom")
    core = lax.rem(my_dom, 2)
    odd = lax.rem(my_slab, 2) == 1
    upper = lax.rem(lax.div(my_slab, 2), 2) == 1
    early = lax.rem(lax.div(my_slab, 4), 8) < 4
    return core, (my_dom - core) * RY, odd, upper, early


def send_kernel(x_ref, early_ref, outer_ref):
    core, top_row, odd, upper, early = where_am_i()
    make_message(x_ref, core, top_row, upper, odd, outer_ref, True)
    make_message(x_ref, core, top_row, jnp.logical_not(upper), jnp.logical_not(odd), early_ref, early)


def late_kernel(x_ref, late_ref):
    core, top_row, odd, upper, early = where_am_i()
    late = jnp.logical_not(early)
    make_message(x_ref, core, top_row, jnp.logical_not(upper), jnp.logical_not(odd), late_ref, late)


def own_kernel(x_ref, own_ref, part_ref):
    core, top_row, _, _, _ = where_am_i()
    cells = deposit(x_ref, top_row, False)
    st = Stencil(top_row)
    for m in range(MOM):
        g = st.planes(cells, m)
        flats = [st.flat(f) for f in g]
        once = [st.kept(flats[0] + diffusion * g[1])]
        once.append(st.kept(flats[1] + diffusion * (g[0] + g[2])))
        once.append(st.kept(flats[2] + diffusion * (g[1] + g[3])))
        once.append(st.kept(flats[3] + diffusion * g[2]))
        for p in range(2):
            f = st.flat(once[1 + p]) + diffusion * (once[p] + once[2 + p])
            part_ref[m, p, 0] = f[0:RY]
            part_ref[m, p, 1] = f[RY : 2 * RY]
    own_ref[...] = part_ref[:, :, core]


def join_kernel(early_ref, outer_ref, late_ref, own_ref, mine_ref, other_ref):
    core = lax.rem(lax.axis_index("dom"), 2)
    refs = (early_ref, outer_ref, late_ref)
    tops = [[ref[4 * MOM + k].astype(jnp.float32) for k in range(2)] for ref in refs]
    for m in range(MOM):
        at = m % RY
        scales = [1.0 / fixed_factor(top[m // RY][at : at + 1]) for top in tops]
        for p in range(2):

            def arrived(h):
                parts = [ref[4 * m + 2 * h + p].astype(jnp.float32) * c for ref, c in zip(refs, scales)]
                return parts[0] + parts[1] + parts[2]

            other_ref[m, p] = arrived(1 - core)
            mine_ref[m, p] = own_ref[m, p] + arrived(core)


def swap_pairs(n_slabs, n_doms, odd_up, chosen):
    pairs = []
    for s in range(n_slabs):
        for d in range(n_doms):
            if not chosen(s):
                continue
            if d % 2 == 1:
                t = s + 1 if s % 2 == odd_up else s - 1
            else:
                t = s + 2 if (s // 2) % 2 == odd_up else s - 2
            pairs.append((d * n_slabs + s, d * n_slabs + t % n_slabs))
    return pairs


limited = pltpu.CompilerParams(vmem_limit_bytes=16 * 1024 * 1024)
alone = pltpu.CompilerParams(vmem_limit_bytes=60 * 1024 * 1024)
smem = pl.BlockSpec(memory_space=pltpu.SMEM)
hbm = pl.BlockSpec(memory_space=pltpu.HBM)
vmem = pl.BlockSpec(memory_space=pltpu.VMEM)


def make_terms(weights, moments, block_tile, block_slab, block_count):
    return pl.pallas_call(
        terms_kernel,
        out_shape=pltpu.VMEM((ROWS, COLS), jnp.int16),
        in_specs=[smem] + [hbm] * 4,
        out_specs=vmem,
        scratch_shapes=[
            pltpu.VMEM((1, BLK), jnp.int32),
            pltpu.VMEM((1, BLK), jnp.int32),
            pltpu.VMEM((BLK, TC, NZ), jnp.bfloat16),
            pltpu.VMEM((MOM, BLK, NZ), jnp.bfloat16),
            pltpu.VMEM((8 * BLK, NZ), jnp.float32),
            pltpu.VMEM((16 * BLK, NZ), jnp.float32),
            pltpu.SemaphoreType.DMA((CHUNKS + 3,)),
        ],
        compiler_params=alone,
        name="terms",
    )(block_count, block_tile, block_slab, weights[0], moments[0].transpose(1, 0, 2))


message = jax.ShapeDtypeStruct((4 * MOM + 2, RY, NZ), jnp.int16)
part = jax.ShapeDtypeStruct((MOM, 2, RY, NZ), jnp.float32)


def make_send(gathered):
    return pl.pallas_call(
        send_kernel,
        out_shape=(message, message),
        in_specs=[vmem],
        out_specs=(vmem, vmem),
        compiler_params=limited,
        name="send",
    )(gathered)


def make_late(gathered):
    return pl.pallas_call(
        late_kernel,
        out_shape=message,
        in_specs=[vmem],
        out_specs=vmem,
        compiler_params=limited,
        cost_estimate=pl.CostEstimate(flops=400_000_000, bytes_accessed=8_000_000, transcendentals=0),
        name="late",
    )(gathered)


def make_own(gathered):
    return pl.pallas_call(
        own_kernel,
        out_shape=part,
        in_specs=[vmem],
        out_specs=vmem,
        scratch_shapes=[pltpu.VMEM((MOM, 2, 2, RY, NZ), jnp.float32)],
        compiler_params=limited,
        cost_estimate=pl.CostEstimate(flops=400_000_000, bytes_accessed=8_000_000, transcendentals=0),
        name="own",
    )(gathered)


def local(weights, moments, block_tile, block_slab, block_count):
    n_slabs = lax.axis_size("slab")
    n_doms = lax.axis_size("dom")
    x = make_terms(weights, moments, block_tile, block_slab, block_count)
    gathered = lax.all_gather(x, "dom", tiled=True)
    early, outer = make_send(gathered)
    late = make_late(gathered)
    own = make_own(gathered)
    both = ("dom", "slab")
    half = lambda low: lambda s: ((s // 4) % 8 < 4) == low
    early = lax.ppermute(early, both, swap_pairs(n_slabs, n_doms, 0, half(True)))
    outer = lax.ppermute(outer, both, swap_pairs(n_slabs, n_doms, 1, lambda s: True))
    late = lax.ppermute(late, both, swap_pairs(n_slabs, n_doms, 0, half(False)))
    early, outer, late, own = lax.optimization_barrier((early, outer, late, own))
    mine, other = pl.pallas_call(
        join_kernel,
        out_shape=(part, part),
        in_specs=[vmem] * 4,
        out_specs=(vmem, vmem),
        compiler_params=limited,
        name="join",
    )(early, outer, late, own)
    other = lax.ppermute(other, "dom", [(i, i ^ 1) for i in range(n_doms)])
    return mine + other


def solution(mesh):
    return jax.shard_map(
        local,
        mesh=mesh,
        in_specs=(
            P("slab", "dom", None, None),
            P("slab", "dom", None, None),
            P("slab", "dom"),
            P("slab", "dom"),
            P("slab", "dom"),
        ),
        out_specs=P(None, "slab", "dom", None),
        check_vma=False,
    )
```

```python
import functools

import jax
import jax.numpy as jnp
from jax import lax
from jax.experimental import pallas as pl
from jax.experimental.pallas import tpu as pltpu
from jax.sharding import PartitionSpec as P

MOM = 10
BLK = 32
TC = 64
NZ = 128
NY = 64
RY = 8
CHIP_ROWS = 2 * RY
HALO = 4
WIN = CHIP_ROWS + 2 * HALO
PLANES = 4
ROWS = 40
COLS = MOM * TC
KEPT = 8 * BLK
CHUNKS = 1
GROUP = 4
diffusion = 0.16
keep_weight = 1.0 - 6.0 * diffusion


def iota(shape, dim):
    return lax.broadcasted_iota(jnp.int32, shape, dim)


def fixed_factor(top):
    return jnp.exp2(14.9 - top)


def power(exponent):
    return jnp.exp2(exponent).astype(jnp.bfloat16).astype(jnp.float32)


def terms_kernel(
    count_ref, tile_hbm, slab_hbm, weight_hbm, moment_hbm, out_ref,
    tile_ref, slab_ref, weight_ref, moment_ref, term_ref, mom_ref, sems,
):
    my_slab, my_dom, n_slabs = lax.axis_index("slab"), lax.axis_index("dom"), lax.axis_size("slab")
    size = BLK // CHUNKS
    small = [
        pltpu.make_async_copy(moment_hbm, moment_ref, sems.at[CHUNKS]),
        pltpu.make_async_copy(tile_hbm, tile_ref, sems.at[CHUNKS + 1]),
        pltpu.make_async_copy(slab_hbm, slab_ref, sems.at[CHUNKS + 2]),
    ]
    copies = []
    for c in range(CHUNKS):
        part = pl.ds(c * size, size)
        copies.append(pltpu.make_async_copy(weight_hbm.at[part], weight_ref.at[part], sems.at[c]))
    for copy in small + copies:
        copy.start()
    for copy in small:
        copy.wait()
    for m in range(MOM):
        mom_ref[BLK * m : BLK * (m + 1), :] = moment_ref[m].astype(jnp.float32)
    mom_ref[BLK * MOM :, :] = jnp.zeros((BLK * (16 - MOM), NZ), jnp.float32)
    tile, slab = tile_ref[...], slab_ref[...]
    step = slab - my_slab
    step = jnp.where(step == n_slabs - 1, -1, jnp.where(step == 1 - n_slabs, 1, step))
    plane = 1 + lax.shift_right_logical(tile, 7) + 2 * step
    row = lax.shift_right_logical(tile & 127, 1)
    used = iota((1, BLK), 1) < count_ref[0, 0]
    code = jnp.where(used, plane * NY + row + 1, 0).astype(jnp.float32)
    half = (tile & 1).astype(jnp.float32)
    both = jnp.where(iota((8, BLK), 0) == 0, code, half).astype(jnp.bfloat16)
    slot = iota((BLK, COLS), 0)
    slot = lax.shift_right_logical(slot, 1) + (slot & 1) * (BLK // 2)
    lane = iota((BLK, COLS), 1) - my_dom * BLK
    spread = jnp.where(lane == slot, 1.0, 0.0).astype(jnp.bfloat16)
    codes = jnp.dot(both, spread, preferred_element_type=jnp.float32)
    low_half = iota((16, NZ), 1) < TC
    for b in range(0, BLK, GROUP):
        if b % size == 0:
            copies[b // size].wait()
        moms = [mom_ref[pl.ds(b + i, 16, stride=BLK), :] for i in range(GROUP)]
        mom = jnp.concatenate(moms, axis=0).astype(jnp.bfloat16)
        w = weight_ref[b : b + GROUP].reshape(GROUP * TC, NZ)
        term = lax.dot_general(mom, w, (((1,), (1,)), ((), ())), preferred_element_type=jnp.float32)
        for i in range(0, GROUP, 2):
            cols = slice(TC * i, TC * (i + 2))
            pair = jnp.where(low_half, term[16 * i : 16 * i + 16, cols], term[16 * i + 16 : 16 * i + 32, cols])
            term_ref[8 * (b + i) : 8 * (b + i) + 16, :] = pair
    terms = []
    for j in range(MOM // 2):
        even = term_ref[pl.ds(2 * j, BLK // 2, stride=16), :]
        odd = term_ref[pl.ds(2 * j + 1, BLK // 2, stride=16), :]
        rows = (
            jnp.where(low_half, even, pltpu.roll(odd, TC, 1)),
            jnp.where(low_half, pltpu.roll(even, TC, 1), odd),
        )
        terms.append(jnp.concatenate(rows, axis=0))
    top = functools.reduce(jnp.maximum, [jnp.abs(term) for term in terms])
    top = jnp.max(top, axis=1, keepdims=True)
    top = jnp.floor(jnp.log2(jnp.maximum(top, 1e-33))) + 1.0
    factor = power(15.0 - top)
    for j, term in enumerate(terms):
        q = jnp.clip(jnp.floor(term * factor + 0.5), -32767.0, 32767.0)
        out_ref[0:BLK, NZ * j : NZ * (j + 1)] = q.astype(jnp.int32).astype(jnp.int16)
    tops = jnp.sum(jnp.where(lane == iota((BLK, COLS), 0), top, 0.0), axis=0, keepdims=True)
    codes = jnp.where(iota((8, COLS), 0) == 2, tops, codes)
    out_ref[BLK:ROWS, :] = codes.astype(jnp.int32).astype(jnp.int16)


def gathered_codes(x_ref):
    codes = functools.reduce(
        jnp.add, [x_ref[ROWS * k + BLK : ROWS * (k + 1), :KEPT].astype(jnp.int32) for k in range(8)]
    )
    code = codes[0:1, :] - 1
    scale = power(codes[2:3, :].astype(jnp.float32) - 15.0)
    return code, lax.shift_right_arithmetic(code, 6), code & (NY - 1), codes[1:2, :], scale


def gather_cells(x_ref, spot, scale, count):
    chosen = jnp.where(iota((count, KEPT), 0) == spot, scale, 0.0)
    chosen = jnp.concatenate([256.0 * chosen, chosen], axis=1).astype(jnp.bfloat16)
    terms = [x_ref[ROWS * k : ROWS * k + BLK, :].astype(jnp.int32) for k in range(8)]
    high = [lax.shift_right_arithmetic(q, 8).astype(jnp.float32).astype(jnp.bfloat16) for q in terms]
    low = [(q & 255).astype(jnp.float32).astype(jnp.bfloat16) for q in terms]
    return jnp.dot(chosen, jnp.concatenate(high + low, axis=0), preferred_element_type=jnp.float32)


def deposit(x_ref, top_row, flip):
    code, plane, row, half, scale = gathered_codes(x_ref)
    if flip is not False:
        plane = jnp.where(flip, PLANES - 1 - plane, plane)
    rel = row - top_row
    valid = (code >= 0) & (rel >= -HALO) & (rel < CHIP_ROWS + HALO)
    spot = (half * PLANES + plane) * WIN + jnp.where(rel < 0, rel + WIN, rel)
    return gather_cells(x_ref, jnp.where(valid, spot, -1), scale, 2 * PLANES * WIN)


class Stencil:
    def __init__(self, top_row):
        self.lane = iota((WIN, NZ), 1)
        ring = iota((WIN, NZ), 0)
        at_row = top_row + jnp.where(ring < CHIP_ROWS + HALO, ring, ring - WIN)
        self.inside = (at_row >= 0) & (at_row < NY)

    def planes(self, cells, m):
        chunk = slice(NZ * (m // 2), NZ * (m // 2 + 1))
        out = []
        for q in range(PLANES):
            lower = cells[WIN * q : WIN * (q + 1), chunk]
            upper = cells[WIN * (PLANES + q) : WIN * (PLANES + q + 1), chunk]
            if m % 2 == 0:
                upper = pltpu.roll(upper, TC, 1)
            else:
                lower = pltpu.roll(lower, TC, 1)
            out.append(jnp.where(self.lane < TC, lower, upper))
        return out

    def flat(self, f):
        z = jnp.where(self.lane == 0, 0.0, pltpu.roll(f, 1, 1)) + jnp.where(
            self.lane == NZ - 1, 0.0, pltpu.roll(f, NZ - 1, 1)
        )
        y = pltpu.roll(f, 1, 0) + pltpu.roll(f, WIN - 1, 0)
        return keep_weight * f + diffusion * (y + z)

    def kept(self, f):
        return jnp.where(self.inside, f, 0.0)


def quantize(values_of, ref):
    sub = iota((RY, NZ), 0)
    tops = [jnp.zeros((RY, NZ), jnp.float32)] * 2
    for m in range(MOM):
        values = values_of(m)
        top = functools.reduce(jnp.maximum, [jnp.abs(v) for v in values])
        for k in (4, 2, 1):
            top = jnp.maximum(top, pltpu.roll(top, k, 0))
        top = jnp.floor(jnp.log2(jnp.maximum(top, 1e-33))) + 1.0
        factor = fixed_factor(top)
        tops[m // RY] = jnp.where(sub == m % RY, top, tops[m // RY])
        for k, v in enumerate(values):
            ref[4 * m + k] = jnp.floor(v * factor + 0.5).astype(jnp.int32).astype(jnp.int16)
    for k in range(2):
        ref[4 * MOM + k] = tops[k].astype(jnp.int32).astype(jnp.int16)


def make_message(x_ref, core, top_row, far_up, near_up, ref, active):
    @pl.when(active & (core == 1))
    def _():
        cells = deposit(x_ref, top_row, near_up)
        st = Stencil(top_row)

        def values_of(m):
            g0, g1, g2, _ = st.planes(cells, m)
            l0 = st.flat(g0)
            once0 = st.kept(l0 + diffusion * g1)
            once1 = st.kept(st.flat(g1) + diffusion * (g0 + g2))
            outer = diffusion * (l0 + once0)
            inner = st.flat(once0) + diffusion * (diffusion * g0 + once1)
            first = jnp.where(near_up, inner, outer)
            second = jnp.where(near_up, outer, inner)
            return [f[RY * h : RY * (h + 1)] for h in range(2) for f in (first, second)]

        quantize(values_of, ref)

    @pl.when(active & (core == 0))
    def _():
        code, plane, row, half, scale = gathered_codes(x_ref)
        rel = row - top_row
        wanted = jnp.where(far_up, PLANES - 1, 0)
        valid = (code >= 0) & (plane == wanted) & (rel >= 0) & (rel < CHIP_ROWS)
        spot = jnp.where(valid, half * CHIP_ROWS + rel, -1)
        cells = gather_cells(x_ref, spot, scale, 2 * CHIP_ROWS)
        lane = iota((CHIP_ROWS, NZ), 1)

        def values_of(m):
            chunk = slice(NZ * (m // 2), NZ * (m // 2 + 1))
            lower, upper = cells[:CHIP_ROWS, chunk], cells[CHIP_ROWS:, chunk]
            if m % 2 == 0:
                upper = pltpu.roll(upper, TC, 1)
            else:
                lower = pltpu.roll(lower, TC, 1)
            f = diffusion * diffusion * jnp.where(lane < TC, lower, upper)
            pair = (jnp.where(far_up, f, 0.0), jnp.where(far_up, 0.0, f))
            return [g[RY * h : RY * (h + 1)] for h in range(2) for g in pair]

        quantize(values_of, ref)


def where_am_i():
    my_slab, my_dom = lax.axis_index("slab"), lax.axis_index("dom")
    core = lax.rem(my_dom, 2)
    odd = lax.rem(my_slab, 2) == 1
    upper = lax.rem(lax.div(my_slab, 2), 2) == 1
    early = lax.rem(lax.div(my_slab, 4), 8) < 1
    return core, (my_dom - core) * RY, odd, upper, early


def send_kernel(x_ref, early_ref, outer_ref):
    core, top_row, odd, upper, early = where_am_i()
    make_message(x_ref, core, top_row, upper, odd, outer_ref, True)
    make_message(x_ref, core, top_row, jnp.logical_not(upper), jnp.logical_not(odd), early_ref, early)


def late_kernel(x_ref, late_ref):
    core, top_row, odd, upper, early = where_am_i()
    late = jnp.logical_not(early)
    make_message(x_ref, core, top_row, jnp.logical_not(upper), jnp.logical_not(odd), late_ref, late)


def own_kernel(x_ref, own_ref, part_ref):
    core, top_row, _, _, _ = where_am_i()
    cells = deposit(x_ref, top_row, False)
    st = Stencil(top_row)
    for m in range(MOM):
        g = st.planes(cells, m)
        flats = [st.flat(f) for f in g]
        once = [st.kept(flats[0] + diffusion * g[1])]
        once.append(st.kept(flats[1] + diffusion * (g[0] + g[2])))
        once.append(st.kept(flats[2] + diffusion * (g[1] + g[3])))
        once.append(st.kept(flats[3] + diffusion * g[2]))
        for p in range(2):
            f = st.flat(once[1 + p]) + diffusion * (once[p] + once[2 + p])
            part_ref[m, p, 0] = f[0:RY]
            part_ref[m, p, 1] = f[RY : 2 * RY]
    own_ref[...] = part_ref[:, :, core]


def join_kernel(early_ref, outer_ref, late_ref, own_ref, mine_ref, other_ref):
    core = lax.rem(lax.axis_index("dom"), 2)
    refs = (early_ref, outer_ref, late_ref)
    tops = [[ref[4 * MOM + k].astype(jnp.float32) for k in range(2)] for ref in refs]
    for m in range(MOM):
        at = m % RY
        scales = [1.0 / fixed_factor(top[m // RY][at : at + 1]) for top in tops]
        for p in range(2):

            def arrived(h):
                parts = [ref[4 * m + 2 * h + p].astype(jnp.float32) * c for ref, c in zip(refs, scales)]
                return parts[0] + parts[1] + parts[2]

            other_ref[m, p] = arrived(1 - core)
            mine_ref[m, p] = own_ref[m, p] + arrived(core)


def swap_pairs(n_slabs, n_doms, odd_up, chosen):
    pairs = []
    for s in range(n_slabs):
        for d in range(n_doms):
            if not chosen(s):
                continue
            if d % 2 == 1:
                t = s + 1 if s % 2 == odd_up else s - 1
            else:
                t = s + 2 if (s // 2) % 2 == odd_up else s - 2
            pairs.append((d * n_slabs + s, d * n_slabs + t % n_slabs))
    return pairs


limited = pltpu.CompilerParams(vmem_limit_bytes=16 * 1024 * 1024)
alone = pltpu.CompilerParams(vmem_limit_bytes=60 * 1024 * 1024)
smem = pl.BlockSpec(memory_space=pltpu.SMEM)
hbm = pl.BlockSpec(memory_space=pltpu.HBM)
vmem = pl.BlockSpec(memory_space=pltpu.VMEM)


def make_terms(weights, moments, block_tile, block_slab, block_count):
    return pl.pallas_call(
        terms_kernel,
        out_shape=pltpu.VMEM((ROWS, COLS), jnp.int16),
        in_specs=[smem] + [hbm] * 4,
        out_specs=vmem,
        scratch_shapes=[
            pltpu.VMEM((1, BLK), jnp.int32),
            pltpu.VMEM((1, BLK), jnp.int32),
            pltpu.VMEM((BLK, TC, NZ), jnp.bfloat16),
            pltpu.VMEM((MOM, BLK, NZ), jnp.bfloat16),
            pltpu.VMEM((8 * BLK, NZ), jnp.float32),
            pltpu.VMEM((16 * BLK, NZ), jnp.float32),
            pltpu.SemaphoreType.DMA((CHUNKS + 3,)),
        ],
        compiler_params=alone,
        name="terms",
    )(block_count, block_tile, block_slab, weights[0], moments[0].transpose(1, 0, 2))


message = jax.ShapeDtypeStruct((4 * MOM + 2, RY, NZ), jnp.int16)
part = jax.ShapeDtypeStruct((MOM, 2, RY, NZ), jnp.float32)


def make_send(gathered):
    return pl.pallas_call(
        send_kernel,
        out_shape=(message, message),
        in_specs=[vmem],
        out_specs=(vmem, vmem),
        compiler_params=limited,
        name="send",
    )(gathered)


def make_late(gathered):
    return pl.pallas_call(
        late_kernel,
        out_shape=message,
        in_specs=[vmem],
        out_specs=vmem,
        compiler_params=limited,
        cost_estimate=pl.CostEstimate(flops=400_000_000, bytes_accessed=8_000_000, transcendentals=0),
        name="late",
    )(gathered)


def make_own(gathered):
    return pl.pallas_call(
        own_kernel,
        out_shape=part,
        in_specs=[vmem],
        out_specs=vmem,
        scratch_shapes=[pltpu.VMEM((MOM, 2, 2, RY, NZ), jnp.float32)],
        compiler_params=limited,
        cost_estimate=pl.CostEstimate(flops=400_000_000, bytes_accessed=8_000_000, transcendentals=0),
        name="own",
    )(gathered)


def local(weights, moments, block_tile, block_slab, block_count):
    n_slabs = lax.axis_size("slab")
    n_doms = lax.axis_size("dom")
    x = make_terms(weights, moments, block_tile, block_slab, block_count)
    gathered = lax.all_gather(x, "dom", tiled=True)
    early, outer = make_send(gathered)
    late = make_late(gathered)
    own = make_own(gathered)
    both = ("dom", "slab")
    half = lambda low: lambda s: ((s // 4) % 8 < 1) == low
    early = lax.ppermute(early, both, swap_pairs(n_slabs, n_doms, 0, half(True)))
    outer = lax.ppermute(outer, both, swap_pairs(n_slabs, n_doms, 1, lambda s: True))
    late = lax.ppermute(late, both, swap_pairs(n_slabs, n_doms, 0, half(False)))
    early, outer, late, own = lax.optimization_barrier((early, outer, late, own))
    mine, other = pl.pallas_call(
        join_kernel,
        out_shape=(part, part),
        in_specs=[vmem] * 4,
        out_specs=(vmem, vmem),
        compiler_params=limited,
        name="join",
    )(early, outer, late, own)
    other = lax.ppermute(other, "dom", [(i, i ^ 1) for i in range(n_doms)])
    return mine + other


def solution(mesh):
    return jax.shard_map(
        local,
        mesh=mesh,
        in_specs=(
            P("slab", "dom", None, None),
            P("slab", "dom", None, None),
            P("slab", "dom"),
            P("slab", "dom"),
            P("slab", "dom"),
        ),
        out_specs=P(None, "slab", "dom", None),
        check_vma=False,
    )
```
